32 devices in a mesh: wide: 8 (over z, core), narrow: 4 (over y, x).
Axes of the slice: x: 2, y: 2, z: 4, core: 2. Of those that a mesh axis runs over, the one named last changes fastest.
Arguments:
- tokens: bfloat16 [16384, 2048], P('wide', 'narrow'), may hold values from -65 to 65
- segment_ids: int32 [16384], P('wide'), may hold values from 0 to 15, never falling along the last dimension, each value on 1 to 2000 neighbouring positions
- norm1_gain: float32 [2048], replicated, may hold values from 0.25 to 1.75
- in_weight: bfloat16 [2048, 3, 2048], P('wide', None, 'narrow'), may hold values from -0.125 to 0.125
- conv_weight: float32 [3, 2048], replicated, may hold values from -3 to 3
- out_weight: bfloat16 [2048, 2048], P('narrow', 'wide'), may hold values from -0.125 to 0.125
- norm2_gain: float32 [2048], replicated, may hold values from 0.25 to 1.75
- gate_weight: bfloat16 [2048, 8192], P('wide', 'narrow'), may hold values from -0.125 to 0.125
- up_weight: bfloat16 [2048, 8192], P('wide', 'narrow'), may hold values from -0.125 to 0.125
- down_weight: bfloat16 [8192, 2048], P('narrow', 'wide'), may hold values from -0.0625 to 0.0625
- cotangent: bfloat16 [16384, 2048], P('wide', 'narrow'), may hold values from -65 to 65
Outputs:
- block_out: bfloat16 [16384, 2048], P('wide', 'narrow')
- tokens_grad: bfloat16 [16384, 2048], P('wide', 'narrow')
- norm1_gain_grad: float32 [2048], P('narrow')
- in_weight_grad: float32 [2048, 3, 2048], P('wide', None, 'narrow')
- conv_weight_grad: float32 [3, 2048], P(None, 'narrow')
- out_weight_grad: float32 [2048, 2048], P('narrow', 'wide')
- norm2_gain_grad: float32 [2048], P('narrow')
- gate_weight_grad: float32 [2048, 8192], P('wide', 'narrow')
- up_weight_grad: float32 [2048, 8192], P('wide', 'narrow')
- down_weight_grad: float32 [8192, 2048], P('narrow', 'wide')
The draws below stay inside these ranges and needn't reach their ends.
Inputs may be any that keep to these rules, and one draw needn't show every extreme that they name: `segment_ids`: along the tokens the segment ids never fall; each segment holds 1 to 2000 tokens, and one holds exactly 2000.
All inputs are finite; a program needn't handle non-finite values.
Results may differ from the reference program's by a relative error of at most 0.008.
Values may be sent and summed in bfloat16 or wider, within the bound.
A program may use at most 384 MiB of HBM per device.

```python
import math
import jax
import jax.numpy as jnp
import numpy as np
from jax import lax

D = 2048
FF = 8192
CONV = 3
TOK_DEV = 2048
DOC_MOST = 2000
TOKENS = 16384
DOCS = 16


def scaled_field(key, row_count, col_count):
    key_base, key_rows, key_cols = jax.random.split(key, 3)
    row_place = jnp.arange(row_count, dtype=jnp.float32) / row_count
    col_place = jnp.arange(col_count, dtype=jnp.float32) / col_count
    row_noise = jax.random.uniform(key_rows, (row_count,), dtype=jnp.float32) - 0.5
    col_noise = jax.random.uniform(key_cols, (col_count,), dtype=jnp.float32) - 0.5
    row_scale = 10.0 ** (0.5 * row_place - 0.25 + 0.5 * row_noise)
    col_scale = 0.5 * 10.0 ** (0.8 * col_place + 0.2 * col_noise)
    base = jnp.clip(jax.random.normal(key_base, (row_count, col_count), dtype=jnp.float32), -5.0, 5.0)
    return base * row_scale[:, None] * col_scale[None, :]


def draw_tokens(key, part):
    return scaled_field(jax.random.fold_in(key, 11), TOKENS, D).astype(jnp.bfloat16)


def draw_cotangent(key, part):
    return scaled_field(jax.random.fold_in(key, 23), TOKENS, D).astype(jnp.bfloat16)


def levels(key, dims, cuts, least, top_value):
    gain = 1.0
    for dim, parts in cuts:
        steps = jax.random.uniform(jax.random.fold_in(jax.random.fold_in(key, 6), dim), (parts,), jnp.float32, least / len(cuts), top_value / len(cuts))
        gain = gain * jnp.repeat(jnp.exp(steps), dims[dim] // parts).reshape((-1,) + (1,) * (len(dims) - 1 - dim))
    return gain


def length_profile(number_of, total, limit, skew):
    loads = [(1 << 20) // math.isqrt(standing ** skew) + 1 for standing in range(2, number_of + 1)]
    spare, holding = total - limit - (number_of - 1), [1] * (number_of - 1)
    while spare > 0:
        free = [i for i in range(number_of - 1) if holding[i] < limit]
        mass, budget = sum([loads[i] for i in free]), spare
        for i in free:
            extra = min(limit - holding[i], max(1, budget * loads[i] // mass), spare)
            holding[i] = holding[i] + extra
            spare = spare - extra
    return np.array([limit] + holding)


def uneven(key, amount, total, limit, skew):
    if amount == 2:
        one = jax.random.randint(key, (), max(1, total - limit), min(limit, total - 1) + 1)
        return jnp.stack([one, total - one])
    sizes = jnp.asarray(length_profile(amount, total, limit, skew), jnp.int32)
    twos = (amount - 1) // 2
    source_of, receiver = sizes[1:1 + 2 * twos:2], sizes[2:2 + 2 * twos:2]
    margin = jnp.minimum(source_of - 1, limit - receiver)
    shifted = jax.random.randint(jax.random.fold_in(key, 1), (twos,), 0, 1 << 20) % (margin + 1)
    sizes = sizes.at[1:1 + 2 * twos:2].set(source_of - shifted).at[2:2 + 2 * twos:2].set(receiver + shifted)
    return sizes[jax.random.permutation(jax.random.fold_in(key, 2), amount)]


def scatter_about(stream_key, extent, spread, reach, cuts=(), kind=jnp.bfloat16):
    level = levels(stream_key, extent, cuts, -0.22, 0.18) if cuts else 1.0
    entries = jax.random.normal(stream_key, extent, jnp.float32) * spread * level
    return jnp.minimum(jnp.maximum(entries, -reach), reach).astype(kind)


def setup_inputs(seed: int = 0) -> dict:
    key_list = jax.random.split(jax.random.key(seed), 12)
    return {
        "tokens": draw_tokens(jax.random.fold_in(key_list[11], 71), 0),
        "segment_ids": jnp.searchsorted(jnp.cumsum(uneven(key_list[1], DOCS, TOKENS, DOC_MOST, 0)), jnp.arange(TOKENS), side="right").astype(jnp.int32),
        "norm1_gain": jnp.clip(1.0 + 0.15 * jax.random.normal(key_list[2], (D,), jnp.float32), 0.25, 1.75),
        "in_weight": scatter_about(key_list[3], (D, 3, D), D ** -0.5, 0.125, ((0, 8), (2, 4))),
        "conv_weight": scatter_about(key_list[4], (CONV, D), 0.6, 3.0, (), jnp.float32),
        "out_weight": scatter_about(key_list[5], (D, D), D ** -0.5, 0.125, ((0, 4), (1, 8))),
        "norm2_gain": jnp.clip(1.0 + 0.15 * jax.random.normal(key_list[6], (D,), jnp.float32), 0.25, 1.75),
        "gate_weight": scatter_about(key_list[7], (D, FF), D ** -0.5, 0.125, ((0, 8), (1, 4))),
        "up_weight": scatter_about(key_list[8], (D, FF), D ** -0.5, 0.125, ((0, 8), (1, 4))),
        "down_weight": scatter_about(key_list[9], (FF, D), FF ** -0.5, 0.0625, ((0, 4), (1, 8))),
        "cotangent": draw_cotangent(jax.random.fold_in(key_list[11], 71), 0),
    }


EPSILON = 1e-05
HIGHEST = lax.Precision.HIGHEST

@jax.custom_vjp
def low(v):
    return lax.optimization_barrier(v.astype(jnp.bfloat16)).astype(jnp.float32)

@jax.custom_vjp
def low_back(v):
    return v

def low_keep(v):
    return (low(v), None)

def low_pass(kept, grad):
    return (grad,)

def back_keep(v):
    return (v, None)

def back_low(kept, grad):
    return (low(grad),)
low.defvjp(low_keep, low_pass)
low_back.defvjp(back_keep, back_low)

def product(left, right):
    return jnp.dot(left, right, precision=HIGHEST, preferred_element_type=jnp.float32)

def lagged(values, shift_by):
    head = jnp.zeros((shift_by,) + values.shape[1:], values.dtype)
    return jnp.concatenate([head, values[:values.shape[0] - shift_by]], axis=0)

def forward(params, inputs, segments):
    norm_one, in_proj, kernel, out_proj, norm_two, gate_proj, up_proj, down_proj = params
    length = inputs.shape[0]
    width_all = inputs.shape[1]
    scale_one = lax.rsqrt(lax.optimization_barrier(jnp.mean(inputs * inputs, axis=1, keepdims=True)) + EPSILON)
    normed_one = low(inputs * scale_one * norm_one)
    mixed_proj = low_back(product(normed_one, in_proj.reshape(width_all, 3 * width_all)))
    mixed_proj = mixed_proj.reshape(length, 3, width_all)
    gate_b = mixed_proj[:, 0]
    gate_c = mixed_proj[:, 1]
    values_x = mixed_proj[:, 2]
    gated_in = gate_b * values_x
    positions = jnp.arange(length, dtype=jnp.int32)
    filtered = jnp.zeros_like(gated_in)
    for lag_step in range(CONV):
        keep_mask = ((positions >= lag_step) & (segments == lagged(segments, lag_step))).astype(jnp.float32)
        filtered = filtered + kernel[lag_step] * keep_mask[:, None] * lagged(gated_in, lag_step)
    mixer_out = low(gate_c * filtered)
    branch = low_back(product(mixer_out, out_proj))
    hidden_res = inputs + branch
    scale_two = lax.rsqrt(lax.optimization_barrier(jnp.mean(hidden_res * hidden_res, axis=1, keepdims=True)) + EPSILON)
    normed_two = low(hidden_res * scale_two * norm_two)
    gate_pre = low_back(product(normed_two, gate_proj))
    up_pre = low_back(product(normed_two, up_proj))
    hidden = low(jax.nn.silu(gate_pre) * up_pre)
    return hidden_res + product(hidden, down_proj)

def reference(tokens, segment_ids, norm1_gain, in_weight, conv_weight, out_weight, norm2_gain, gate_weight, up_weight, down_weight, cotangent):
    params = tuple((weight_in.astype(jnp.float32) for weight_in in (norm1_gain, in_weight, conv_weight, out_weight, norm2_gain, gate_weight, up_weight, down_weight)))
    seq_count = TOKENS // TOK_DEV
    inputs = tokens.astype(jnp.float32).reshape(seq_count, TOK_DEV, D)
    segments = segment_ids.astype(jnp.int32).reshape(seq_count, TOK_DEV)
    cot_all = cotangent.astype(jnp.float32).reshape(seq_count, TOK_DEV, D)

    def one_sequence(totals, seq_item):
        seq_in, seq_seg, seq_cot = seq_item

        def apply_block(weights_all, values_in):
            return forward(weights_all, values_in, seq_seg)
        outputs, pull_back = jax.vjp(apply_block, params, seq_in)
        weight_grads, input_grad = pull_back(seq_cot)
        totals = jax.tree.map(lambda left, right: left + right, totals, weight_grads)
        return (totals, (outputs.astype(jnp.bfloat16), input_grad.astype(jnp.bfloat16)))
    zero_grads = jax.tree.map(jnp.zeros_like, params)
    totals, (outputs, input_grads) = lax.scan(one_sequence, zero_grads, (inputs, segments, cot_all))
    block_out = outputs.reshape(TOKENS, D)
    tokens_grad = input_grads.reshape(TOKENS, D)
    return (block_out, tokens_grad, totals[0], totals[1], totals[2], totals[3], totals[4], totals[5], totals[6], totals[7])
```

```python
import functools

import jax
import jax.numpy as jnp
from jax import lax
from jax.experimental import pallas as pl
from jax.experimental.pallas import tpu as pltpu
from jax.sharding import PartitionSpec as P

CONV = 3
EPSILON = 1e-05
BF = jnp.bfloat16
F32 = jnp.float32
TILE = 256
BIG = 512


def contract_rows(left, right):
    return lax.dot_general(left, right, (((0,), (0,)), ((), ())), preferred_element_type=F32)


def contract_cols(left, right):
    return lax.dot_general(left, right, (((1,), (1,)), ((), ())), preferred_element_type=F32)


def lagged(values, shift_by):
    head = jnp.zeros((shift_by,) + values.shape[1:], values.dtype)
    return jnp.concatenate([head, values[: values.shape[0] - shift_by]], axis=0)


ALONG_X = [(0, 1), (1, 0), (2, 3), (3, 2)]
ALONG_Y = [(0, 2), (2, 0), (1, 3), (3, 1)]


def to_x(values):
    return lax.ppermute(values, "narrow", ALONG_X)


def to_y(values):
    return lax.ppermute(values, "narrow", ALONG_Y)


def halves(values, axis):
    middle = values.shape[axis] // 2
    return lax.slice_in_dim(values, 0, middle, axis=axis), lax.slice_in_dim(values, middle, None, axis=axis)


def gather_pieces(block, axis, square, beside=(lambda: (), lambda _: ())):
    if not square:
        first = beside[0]()
        return [lax.all_gather(block, "narrow", axis=axis, tiled=True)], first, beside[1](first)
    from_x, from_y, first = lax.optimization_barrier((to_x(block), to_y(block), beside[0]()))
    low, high, second = lax.optimization_barrier(
        (to_x(halves(from_y, axis)[0]), to_y(halves(from_x, axis)[1]), beside[1](first))
    )
    return [block, from_x, from_y, low, high], first, second


def piece_starts(me, width, square):
    if not square:
        return [0]
    return [me * width, (me ^ 1) * width, (me ^ 2) * width, (me ^ 3) * width, (me ^ 3) * width + width // 2]


def whole(shape):
    return pl.BlockSpec(shape, lambda *_: (0,) * len(shape), pipeline_mode=pl.Buffered(1))


def tiles(width, tile=TILE):
    return pl.BlockSpec((tile, width), lambda i, *_: (i, 0))


def run(kernel, grid, scalars, operands, in_specs, outs, out_specs, scratch=(), flops=0, aliases=None, vmem=56):
    moved = sum(o.size * o.dtype.itemsize for o in operands) + sum(o.size * o.dtype.itemsize for o in outs)
    return pl.pallas_call(
        kernel,
        grid_spec=pltpu.PrefetchScalarGridSpec(
            num_scalar_prefetch=1, grid=grid, in_specs=in_specs, out_specs=out_specs, scratch_shapes=list(scratch)
        ),
        out_shape=outs,
        input_output_aliases=aliases or {},
        cost_estimate=pl.CostEstimate(flops=flops, bytes_accessed=moved, transcendentals=0),
        compiler_params=pltpu.CompilerParams(
            dimension_semantics=("arbitrary",) * len(grid), vmem_limit_bytes=vmem << 20
        ),
    )(scalars, *operands)


def shape_of(shape, dtype):
    return jax.ShapeDtypeStruct(shape, dtype)


def project(me, pieces, square, gain, weight, kernel, masks):
    count = len(pieces)
    row_count = pieces[0].shape[0]
    full, part = weight.shape[0], kernel.shape[1]
    share = full // (4 if square else 1)
    packed = pl.BlockSpec((full, 3 * part), lambda *_: (0, 0), pipeline_mode=pl.Buffered(1))

    def body(me_ref, *refs):
        xs, (gain_ref, w_ref, k_ref, m_ref), (n_ref, x_ref, p_ref, v_ref, y_ref, s_ref), (carry,) = (
            refs[:count],
            refs[count : count + 4],
            refs[count + 4 : count + 10],
            refs[count + 10 :],
        )

        @pl.when(pl.program_id(0) == 0)
        def _():
            carry[...] = jnp.zeros_like(carry)

        values = [ref[...].astype(F32) for ref in xs]
        total = functools.reduce(jnp.add, [jnp.sum(v * v, axis=1, keepdims=True) for v in values])
        scale = lax.rsqrt(total / full + EPSILON)
        s_ref[...] = scale
        for ref, v, start in zip(xs, values, piece_starts(me_ref[0], share, square)):
            at = pl.ds(pl.multiple_of(start, 128), v.shape[1])
            n_ref[:, at] = (v * scale * gain_ref[:, at]).astype(BF)
            x_ref[:, at] = ref[...]
        mixed = jnp.dot(n_ref[...], w_ref[...], preferred_element_type=F32)
        p_ref[...] = mixed
        gated = mixed[:, :part] * mixed[:, 2 * part :]
        row = lax.broadcasted_iota(jnp.int32, gated.shape, 0)
        before, last = carry[6:7, :], carry[7:8, :]
        back_one = jnp.where(row == 0, last, pltpu.roll(gated, 1, 0))
        back_two = jnp.where(row == 0, before, jnp.where(row == 1, last, pltpu.roll(gated, 2, 0)))
        carry[...] = gated[-8:, :]
        keep = m_ref[...]
        filtered = (
            k_ref[0:1, :] * gated + k_ref[1:2, :] * keep[:, 0:1] * back_one + k_ref[2:3, :] * keep[:, 1:2] * back_two
        )
        v_ref[...] = filtered
        y_ref[...] = (mixed[:, part : 2 * part] * filtered).astype(BF)

    return run(
        body,
        (row_count // TILE,),
        me,
        [*pieces, gain, weight, kernel, masks],
        [tiles(p.shape[1]) for p in pieces] + [whole(gain.shape), packed, whole(kernel.shape), tiles(2)],
        [
            shape_of((row_count, full), BF),
            shape_of((row_count, full), BF),
            shape_of((row_count, 3 * part), F32),
            shape_of((row_count, part), F32),
            shape_of((row_count, part), BF),
            shape_of((row_count, 1), F32),
        ],
        [tiles(full), tiles(full), tiles(3 * part), tiles(part), tiles(part), tiles(1)],
        [pltpu.VMEM((8, part), F32)],
        flops=2 * row_count * full * 3 * part,
    )


def mix(core, pieces, mats, x_full, gain):
    count, parts = len(pieces), len(mats)
    row_count, full = x_full.shape
    cols = mats[0].shape[1]

    def body(core_ref, *refs):
        ys, ms, (x_ref, gain_ref), (h_ref, n_ref, s_ref), (all_ref,) = (
            refs[:count],
            refs[count : count + parts],
            refs[count + parts : count + parts + 2],
            refs[count + parts + 2 : count + parts + 5],
            refs[count + parts + 5 :],
        )
        at = 0
        for ref in ys:
            all_ref[:, at : at + ref.shape[1]] = ref[...]
            at += ref.shape[1]
        total = 0.0
        for k, ref in enumerate(ms):
            where = pl.ds(pl.multiple_of((core_ref[0] ^ k) * cols, 128), cols) if parts > 1 else slice(None)
            h = x_ref[:, where].astype(F32) + jnp.dot(all_ref[...], ref[...], preferred_element_type=F32)
            h_ref[:, where] = h
            total = total + jnp.sum(h * h, axis=1, keepdims=True)
        scale = lax.rsqrt(total / full + EPSILON)
        s_ref[...] = scale
        n_ref[...] = (h_ref[...] * scale * gain_ref[...]).astype(BF)

    return run(
        body,
        (row_count // BIG,),
        core,
        [*pieces, *mats, x_full, gain],
        [tiles(p.shape[1], BIG) for p in pieces] + [whole(m.shape) for m in mats] + [tiles(full, BIG), whole(gain.shape)],
        [shape_of((row_count, full), F32), shape_of((row_count, full), BF), shape_of((row_count, 1), F32)],
        [tiles(full, BIG), tiles(full, BIG), tiles(1, BIG)],
        [pltpu.VMEM((BIG, full), BF)],
        flops=2 * row_count * full * full,
    )


def lay(me, pieces, square):
    if not square:
        return pieces[0]
    row_count, share = pieces[0].shape
    full = 4 * share

    def body(me_ref, *refs):
        for ref, start in zip(refs[:-1], piece_starts(me_ref[0], share, True)):
            refs[-1][:, pl.ds(pl.multiple_of(start, 128), ref.shape[1])] = ref[...]

    return run(
        body,
        (row_count // BIG,),
        me,
        pieces,
        [tiles(p.shape[1], BIG) for p in pieces],
        [shape_of((row_count, full), BF)],
        [tiles(full, BIG)],
    )[0]


def expand(me, normed, weight):
    row_count, full = normed.shape
    units = weight.shape[1] // 2

    def body(_, n_ref, w_ref, q_ref, a_ref, b_ref):
        step = min(512, units)
        for at in range(0, units, step):
            gate = jnp.dot(n_ref[...], w_ref[:, at : at + step], preferred_element_type=F32)
            up = jnp.dot(n_ref[...], w_ref[:, units + at : units + at + step], preferred_element_type=F32)
            sig = 1.0 / (1.0 + jnp.exp(-gate))
            active = gate * sig
            q_ref[:, at : at + step] = (active * up).astype(BF)
            a_ref[:, at : at + step] = active.astype(BF)
            b_ref[:, at : at + step] = (up * sig * (1.0 + gate * (1.0 - sig))).astype(BF)

    return run(
        body,
        (row_count // BIG,),
        me,
        [normed, weight],
        [tiles(full, BIG), whole(weight.shape)],
        [shape_of((row_count, units), BF)] * 3,
        [tiles(units, BIG)] * 3,
        flops=2 * row_count * full * 2 * units,
    )


def ffn_back(owners, band, grad, slope_up, slope_gate, down, weight):
    row_count, full = grad.shape
    units = down.shape[0]
    step = min(512, units)
    count = units // step

    def body(_, g_ref, a_ref, b_ref, d_ref, wg_ref, wu_ref, low_ref, high_ref, o_ref, total):
        j = pl.program_id(1)
        dq = contract_cols(g_ref[...], d_ref[...])
        d_gate = (dq * b_ref[...].astype(F32)).astype(BF)
        d_up = (dq * a_ref[...].astype(F32)).astype(BF)
        at = pl.multiple_of(j * step, 128)
        o_ref[:, pl.ds(at, step)] = d_gate
        o_ref[:, pl.ds(units + at, step)] = d_up
        term = contract_cols(d_gate, wg_ref[...]) + contract_cols(d_up, wu_ref[...])

        @pl.when(j == 0)
        def _():
            total[...] = term

        @pl.when(j > 0)
        def _():
            total[...] += term

        @pl.when(j == count - 1)
        def _():
            low_ref[...] = total[:, : full // 2].astype(BF)
            high_ref[...] = total[:, full // 2 :].astype(BF)

    return run(
        body,
        (row_count // band, count),
        owners,
        [grad, slope_up, slope_gate, down, weight, weight],
        [
            pl.BlockSpec((band, full), lambda i, j, o: (o[i], 0)),
            pl.BlockSpec((band, step), lambda i, j, o: (o[i], j)),
            pl.BlockSpec((band, step), lambda i, j, o: (o[i], j)),
            pl.BlockSpec((step, full), lambda i, j, o: (j, 0)),
            pl.BlockSpec((full, step), lambda i, j, o: (0, j)),
            pl.BlockSpec((full, step), lambda i, j, o: (0, count + j)),
        ],
        [shape_of((row_count, full // 2), BF)] * 2 + [shape_of((row_count, 2 * units), BF)],
        [
            pl.BlockSpec((band, full // 2), lambda i, j, o: (i, 0)),
            pl.BlockSpec((band, full // 2), lambda i, j, o: (i, 0)),
            pl.BlockSpec((band, 2 * units), lambda i, j, o: (o[i], 0)),
        ],
        [pltpu.VMEM((band, full), F32)],
        flops=6 * row_count * full * units,
    )


def hidden_back(me, terms, hidden, scale_two, grad, gain):
    band = terms[0][0].shape[0]
    full = gain.shape[1]
    tile = min(TILE, band)
    count = 2 * len(terms)

    def body(_, *refs):
        h_ref, s_ref, g_ref, gain_ref, o_ref, n_ref = refs[count:]

        @pl.when(pl.program_id(0) == 0)
        def _():
            n_ref[...] = jnp.zeros_like(n_ref)

        sums = [functools.reduce(jnp.add, [r[...].astype(F32) for r in refs[k:count:2]]) for k in (0, 1)]
        d_normed = jnp.concatenate(sums, axis=1)
        h, scale = h_ref[...], s_ref[...]
        scaled = d_normed * gain_ref[...]
        inner = jnp.sum(scaled * h, axis=1, keepdims=True) / full
        o_ref[...] = (g_ref[...].astype(F32) + scale * (scaled - h * scale * scale * inner)).astype(BF)
        n_ref[...] += jnp.sum(d_normed * h * scale, axis=0, keepdims=True)

    def mine(width):
        return pl.BlockSpec((tile, width), lambda i, o: (o[0] * (band // tile) + i, 0))

    flat = [half for pair in terms for half in pair]
    return run(
        body,
        (band // tile,),
        me,
        [*flat, hidden, scale_two, grad, gain],
        [tiles(f.shape[1], tile) for f in flat] + [mine(full), mine(1), mine(full), whole(gain.shape)],
        [shape_of((band, full), BF), shape_of((1, full), F32)],
        [tiles(full, tile), pl.BlockSpec((1, full), lambda i, *_: (0, 0))],
    )


def mixer_back(owners, pieces, out_rows, mixed, filtered, kernel, masks, weight):
    part, full = out_rows.shape
    row_count = mixed.shape[0]
    count = row_count // TILE
    size = owners.shape[0]
    band = row_count // size
    given = len(pieces)
    packed = pl.BlockSpec((full, 3 * part), lambda *_: (0, 0), pipeline_mode=pl.Buffered(1))

    def body(own_ref, *refs):
        w_ref, p_ref, v_ref, k_ref, m_ref, r_ref = refs[given : given + 6]
        outs = refs[given + 6 : given + 6 + 2 * size]
        o_ref, kg_ref, d_ref, carry, dy_ref = refs[given + 6 + 2 * size :]
        i = pl.program_id(0)

        @pl.when(i == 0)
        def _():
            carry[...] = jnp.zeros_like(carry)
            kg_ref[...] = jnp.zeros_like(kg_ref)

        first = (count - 1 - i) * TILE
        if given == 1:
            d_ref[...] = refs[0][pl.ds(pl.multiple_of(first, TILE), TILE), :]
        else:
            apart = (first // band) ^ own_ref[size - 1]
            within = pl.multiple_of(first % band, TILE)
            for k in range(3):

                @pl.when(apart == k)
                def _(k=k):
                    d_ref[...] = refs[k][pl.ds(within, TILE), :]

            @pl.when((apart == 3) & (within < band // 2))
            def _():
                d_ref[...] = refs[3][pl.ds(within, TILE), :]

            @pl.when((apart == 3) & (within >= band // 2))
            def _():
                d_ref[...] = refs[4][pl.ds(pl.multiple_of(within - band // 2, TILE), TILE), :]

        dy_ref[...] = contract_cols(d_ref[...], w_ref[...])
        dy = dy_ref[...]
        b, c, x = p_ref[:, :part], p_ref[:, part : 2 * part], p_ref[:, 2 * part :]
        dv = dy * c
        keep = m_ref[...]
        one, two = dv * keep[:, 0:1], dv * keep[:, 1:2]
        row = lax.broadcasted_iota(jnp.int32, dv.shape, 0)
        end = TILE - 1
        next_one = jnp.where(row == end, carry[0:1, :], pltpu.roll(one, TILE - 1, 0))
        next_two = jnp.where(
            row == end, carry[2:3, :], jnp.where(row == end - 1, carry[1:2, :], pltpu.roll(two, TILE - 2, 0))
        )
        carry[0:1, :] = one[0:1, :]
        carry[1:3, :] = two[0:2, :]
        u = b * x
        kg_ref[0:1, :] += jnp.sum(dv * u, axis=0, keepdims=True)
        kg_ref[1:2, :] += jnp.sum(next_one * u, axis=0, keepdims=True)
        kg_ref[2:3, :] += jnp.sum(next_two * u, axis=0, keepdims=True)
        du = k_ref[0:1, :] * dv + k_ref[1:2, :] * next_one + k_ref[2:3, :] * next_two
        o_ref[:, :part] = (du * x).astype(BF)
        o_ref[:, part : 2 * part] = (dy * v_ref[...]).astype(BF)
        o_ref[:, 2 * part :] = (du * b).astype(BF)
        for k in range(size):
            rows = pl.ds(pl.multiple_of(own_ref[k] * part, part), part)
            term = contract_cols(o_ref[...], r_ref[rows, :])
            outs[2 * k][...] = term[:, : part // 2].astype(BF)
            outs[2 * k + 1][...] = term[:, part // 2 :].astype(BF)

    def back(width):
        return pl.BlockSpec((TILE, width), lambda i, *_: (count - 1 - i, 0))

    return run(
        body,
        (count,),
        owners,
        [*pieces, out_rows, mixed, filtered, kernel, masks, weight],
        [whole(p.shape) for p in pieces]
        + [whole(out_rows.shape), back(3 * part), back(part), whole(kernel.shape), back(2), packed],
        [shape_of((row_count, part // 2), BF)] * (2 * size)
        + [shape_of((row_count, 3 * part), BF), shape_of((CONV, part), F32), shape_of((row_count, full), BF)],
        [back(part // 2)] * (2 * size)
        + [back(3 * part), pl.BlockSpec((CONV, part), lambda i, *_: (0, 0)), back(full)],
        [pltpu.VMEM((8, part), F32), pltpu.VMEM((TILE, part), F32)],
        flops=2 * row_count * full * part * 4,
    )


def front_terms(owners, left, right):
    row_count, depth = left.shape
    size = owners.shape[0]
    width = right.shape[1] // size

    def body(own_ref, l_ref, r_ref, *outs):
        for k in range(size):
            at = pl.ds(pl.multiple_of(own_ref[k] * width, width), width)
            term = jnp.dot(l_ref[...], r_ref[:, at], preferred_element_type=F32)
            outs[2 * k][...] = term[:, : width // 2].astype(BF)
            outs[2 * k + 1][...] = term[:, width // 2 :].astype(BF)

    return run(
        body,
        (row_count // BIG,),
        owners,
        [left, right],
        [tiles(depth, BIG), whole(right.shape)],
        [shape_of((row_count, width // 2), BF)] * (2 * size),
        [tiles(width // 2, BIG)] * (2 * size),
        flops=2 * row_count * depth * width * size,
    )


def add_low(left, right):
    return (left.astype(F32) + right.astype(F32)).astype(BF)


def scatter_first(terms):
    return lax.optimization_barrier((to_x(terms[0][0]), to_y(terms[0][1])))


def scatter_last(terms, via_x, via_y):
    to_send = terms[1][0], add_low(terms[1][1], via_y), add_low(terms[2][0], via_x), terms[2][1]
    x_low, x_high, y_low, y_high = lax.optimization_barrier(
        (to_x(to_send[0]), to_x(to_send[1]), to_y(to_send[2]), to_y(to_send[3]))
    )
    return [terms[3], (x_low, x_high), (y_low, y_high)]


def scatter_plain(terms, axis):
    joined = jnp.concatenate([jnp.concatenate(pair, axis=1) for pair in terms], axis=axis).astype(F32)
    return lax.psum_scatter(joined, "narrow", scatter_dimension=axis, tiled=True)


def total_of(pairs):
    return jnp.concatenate(
        [functools.reduce(jnp.add, [pair[k].astype(F32) for pair in pairs]) for k in (0, 1)], axis=1
    )


def wide_all(block, axis):
    return lax.all_gather(block, "wide", axis=axis, tiled=True)


def wide_sums(terms, axis):
    return lax.psum_scatter(terms.astype(BF), "wide", scatter_dimension=axis, tiled=True).astype(F32)


def narrow_total(values, square):
    if not square:
        return lax.psum(values, "narrow")
    values = values + to_x(values)
    return values + to_y(values)


def wide_total(values, square):
    if not square:
        return lax.psum(values, "wide")
    for bit in (1, 2, 4):
        values = values + lax.ppermute(values, "wide", [(i, i ^ bit) for i in range(lax.axis_size("wide"))])
    return values


def after(value, *others):
    return lax.optimization_barrier((value, *others))[0]


def per_device(
    square,
    size,
    tokens,
    segment_ids,
    norm1_gain,
    in_weight,
    conv_weight,
    out_weight,
    norm2_gain,
    gate_weight,
    up_weight,
    down_weight,
    cotangent,
):
    full_width = norm1_gain.shape[0]
    part_width = tokens.shape[1]
    units = gate_weight.shape[1]
    row_count = tokens.shape[0]
    band = row_count // size
    me = lax.axis_index("narrow")
    core = lax.axis_index("wide") % 2
    me_s = me.reshape(1).astype(jnp.int32)
    core_s = core.reshape(1).astype(jnp.int32)
    offset = me * part_width
    kernel = lax.dynamic_slice_in_dim(conv_weight, offset, part_width, 1)
    gain_one, gain_two = norm1_gain[None, :], norm2_gain[None, :]

    order = [me ^ 3, me ^ 1, me ^ 2, me] if square else list(range(size))
    owners = jnp.stack([jnp.asarray(o, jnp.int32) for o in order])

    pack = jnp.concatenate([in_weight[:, k] for k in range(3)] + list(halves(out_weight, 0)), axis=1)
    slim = pack.shape[0]
    if square:
        pack_all = wide_all(pack, 0)
        out_rows = pack_all[:, 3 * part_width :].reshape(-1, slim, 2, slim)
        out_rows = out_rows.transpose(2, 1, 0, 3).reshape(part_width, full_width)
    else:
        pack_all = wide_all(jnp.concatenate([in_weight[:, k] for k in range(3)], axis=1), 0)
        out_rows = wide_all(out_weight, 1)
    x_pieces, _, _ = gather_pieces(tokens, 1, square)
    both_all = wide_all(after(jnp.concatenate([gate_weight, up_weight], axis=1), *x_pieces), 0)

    positions = lax.broadcasted_iota(jnp.int32, (row_count,), 0)
    masks = jnp.stack(
        [((positions >= k) & (segment_ids == lagged(segment_ids, k))).astype(F32) for k in (1, 2)], axis=1
    )
    normed_one, x_full, mixed, filtered, mixer_low, scale_one = project(
        me_s, x_pieces, square, gain_one, pack_all, kernel, masks
    )
    down_all = wide_all(after(down_weight, mixer_low), 1)

    if square:
        half_cols = full_width // 2
        pairs = [(i, i ^ 1) for i in range(lax.axis_size("wide"))]
        out_half = lax.dynamic_slice_in_dim(out_rows, core * half_cols, half_cols, 1)
        out_half = after(out_half, x_pieces[3])
        mine = jnp.concatenate(gather_pieces(out_half, 0, True)[0], axis=0)
        mats = [mine, lax.ppermute(mine, "wide", pairs)]
    else:
        mats = [lax.all_gather(out_rows, "narrow", axis=0, tiled=True)]
    y_pieces, _, _ = gather_pieces(mixer_low, 1, square)
    g_pieces, (hidden, normed_two, scale_two), (hidden_low, slope_up, slope_gate) = gather_pieces(
        after(cotangent, *y_pieces[1:]),
        1,
        square,
        (
            lambda: tuple(mix(core_s, y_pieces, mats, x_full, gain_two)),
            lambda first: tuple(expand(me_s, first[1], both_all)),
        ),
    )
    grad_full = lay(me_s, g_pieces, square)

    down_terms = contract_rows(hidden_low, grad_full).astype(BF)
    down_grad = wide_sums(down_terms, 1)
    low, high, d_both = ffn_back(owners, band, grad_full, after(slope_up, down_terms), slope_gate, down_all, both_all)
    ffn_terms = [(low[k * band : (k + 1) * band], high[k * band : (k + 1) * band]) for k in range(size)]
    if square:
        via_x, via_y = scatter_first(ffn_terms)
        both_terms = contract_rows(normed_two, d_both).astype(BF)
        via_x, via_y, both_terms = lax.optimization_barrier((via_x, via_y, both_terms))
        sums = scatter_last(ffn_terms, via_x, via_y)
    else:
        both_terms = contract_rows(normed_two, d_both).astype(BF)
        sums = [tuple(halves(scatter_plain(ffn_terms, 0), 1))]
    both_grad = wide_sums(after(both_terms, down_grad), 0)
    d_hidden_rows, gain_two_terms = hidden_back(me_s, sums, hidden, scale_two, grad_full, gain_two)
    dh_pieces, out_parts, _ = gather_pieces(
        d_hidden_rows, 0, square, (lambda: tuple(front_terms(owners, hidden_low, down_all)), lambda _: ())
    )
    *one_parts, d_flat, kernel_grad, d_hidden_low = mixer_back(
        owners, dh_pieces, out_rows, mixed, filtered, kernel, masks, pack_all
    )
    one_parts = list(zip(one_parts[0::2], one_parts[1::2]))
    out_parts = list(zip(out_parts[0::2], out_parts[1::2]))
    if square:
        via_x, via_y = scatter_first(one_parts)
        in_terms = contract_rows(normed_one, d_flat).astype(BF)
        via_x, via_y, in_terms = lax.optimization_barrier((via_x, via_y, in_terms))
        one_sums = scatter_last(one_parts, via_x, via_y)
        out_terms = contract_rows(mixer_low, after(d_hidden_low, in_terms)).astype(BF)
        d_normed_one = total_of(one_sums)
        via_x, via_y = scatter_first([tuple(after(out_parts[0], d_normed_one))] + out_parts[1:])
        ffn_out = total_of(scatter_last(out_parts, via_x, via_y))
        in_grad = wide_sums(after(in_terms, both_grad), 0)
        out_grad = wide_sums(after(out_terms, in_grad, ffn_out), 1)
    else:
        in_terms = contract_rows(normed_one, d_flat).astype(BF)
        out_terms = contract_rows(mixer_low, d_hidden_low).astype(BF)
        d_normed_one = scatter_plain(one_parts, 1)
        ffn_out = scatter_plain(out_parts, 1)
        in_grad, out_grad = wide_sums(in_terms, 0), wide_sums(out_terms, 1)
    gate_grad, up_grad = both_grad[:, :units], both_grad[:, units:]
    in_grad = jnp.stack([in_grad[:, k * part_width : (k + 1) * part_width] for k in range(3)], axis=1)
    block_out = (lax.dynamic_slice_in_dim(hidden, offset, part_width, 1) + ffn_out).astype(BF)

    my_gain = lax.dynamic_slice_in_dim(norm1_gain, offset, part_width)
    x_part = tokens.astype(F32)
    scaled_one = d_normed_one * my_gain
    inner_one = narrow_total(jnp.sum(scaled_one * x_part, axis=1).reshape(-1, 128), square)
    inner_one = inner_one.reshape(row_count, 1) / full_width
    tokens_grad = (
        lax.dynamic_slice_in_dim(d_hidden_low, offset, part_width, 1).astype(F32)
        + scale_one * (scaled_one - x_part * scale_one * scale_one * inner_one)
    ).astype(BF)
    gain_one_grad = jnp.sum(d_normed_one * x_part * scale_one, axis=0)
    gain_two_terms = narrow_total(gain_two_terms.reshape(size, part_width), square)
    gain_two_terms = lax.dynamic_slice_in_dim(gain_two_terms, me, 1, 0)
    small = wide_total(jnp.concatenate([gain_one_grad[None, :], gain_two_terms, kernel_grad], axis=0), square)
    gain_one_grad, gain_two_grad, kernel_grad = small[0], small[1], small[2:]
    return (
        block_out,
        tokens_grad,
        gain_one_grad,
        in_grad,
        kernel_grad,
        out_grad,
        gain_two_grad,
        gate_grad,
        up_grad,
        down_grad,
    )


def solution(mesh):
    size = mesh.shape["narrow"]
    square = size == 4 and mesh.shape["wide"] == 8

    def step(*args):
        return per_device(square, size, *args)

    in_specs = (
        P("wide", "narrow"),
        P("wide"),
        P(),
        P("wide", None, "narrow"),
        P(),
        P("narrow", "wide"),
        P(),
        P("wide", "narrow"),
        P("wide", "narrow"),
        P("narrow", "wide"),
        P("wide", "narrow"),
    )
    out_specs = (
        P("wide", "narrow"),
        P("wide", "narrow"),
        P("narrow"),
        P("wide", None, "narrow"),
        P(None, "narrow"),
        P("narrow", "wide"),
        P("narrow"),
        P("wide", "narrow"),
        P("wide", "narrow"),
        P("narrow", "wide"),
    )
    return jax.shard_map(step, mesh=mesh, in_specs=in_specs, out_specs=out_specs, check_vma=False)
```

```python
import functools

import jax
import jax.numpy as jnp
from jax import lax
from jax.experimental import pallas as pl
from jax.experimental.pallas import tpu as pltpu
from jax.sharding import PartitionSpec as P

CONV = 3
EPSILON = 1e-05
BF = jnp.bfloat16
F32 = jnp.float32
TILE = 512
BIG = 512


def contract_rows(left, right):
    return lax.dot_general(left, right, (((0,), (0,)), ((), ())), preferred_element_type=F32)


def contract_cols(left, right):
    return lax.dot_general(left, right, (((1,), (1,)), ((), ())), preferred_element_type=F32)


def lagged(values, shift_by):
    head = jnp.zeros((shift_by,) + values.shape[1:], values.dtype)
    return jnp.concatenate([head, values[: values.shape[0] - shift_by]], axis=0)


ALONG_X = [(0, 1), (1, 0), (2, 3), (3, 2)]
ALONG_Y = [(0, 2), (2, 0), (1, 3), (3, 1)]
ACROSS = [(0, 3), (3, 0), (1, 2), (2, 1)]


def to_x(values):
    return lax.ppermute(values, "narrow", ALONG_X)


def to_y(values):
    return lax.ppermute(values, "narrow", ALONG_Y)


def to_far(values):
    return lax.ppermute(values, "narrow", ACROSS)


def halves(values, axis):
    middle = values.shape[axis] // 2
    return lax.slice_in_dim(values, 0, middle, axis=axis), lax.slice_in_dim(values, middle, None, axis=axis)


def gather_pieces(block, axis, square, beside=(lambda: (), lambda _: ())):
    if not square:
        first = beside[0]()
        return [lax.all_gather(block, "narrow", axis=axis, tiled=True)], first, beside[1](first)
    from_x, from_y, first = lax.optimization_barrier((to_x(block), to_y(block), beside[0]()))
    low, high, second = lax.optimization_barrier(
        (to_x(halves(from_y, axis)[0]), to_y(halves(from_x, axis)[1]), beside[1](first))
    )
    return [block, from_x, from_y, low, high], first, second


def piece_starts(me, width, square):
    if not square:
        return [0]
    return [me * width, (me ^ 1) * width, (me ^ 2) * width, (me ^ 3) * width, (me ^ 3) * width + width // 2]


def whole(shape):
    return pl.BlockSpec(shape, lambda *_: (0,) * len(shape), pipeline_mode=pl.Buffered(1))


def tiles(width, tile=TILE):
    return pl.BlockSpec((tile, width), lambda i, *_: (i, 0))


def run(kernel, grid, scalars, operands, in_specs, outs, out_specs, scratch=(), flops=0, aliases=None, vmem=56):
    moved = sum(o.size * o.dtype.itemsize for o in operands) + sum(o.size * o.dtype.itemsize for o in outs)
    return pl.pallas_call(
        kernel,
        grid_spec=pltpu.PrefetchScalarGridSpec(
            num_scalar_prefetch=1, grid=grid, in_specs=in_specs, out_specs=out_specs, scratch_shapes=list(scratch)
        ),
        out_shape=outs,
        input_output_aliases=aliases or {},
        cost_estimate=pl.CostEstimate(flops=flops, bytes_accessed=moved, transcendentals=0),
        compiler_params=pltpu.CompilerParams(
            dimension_semantics=("arbitrary",) * len(grid), vmem_limit_bytes=vmem << 20
        ),
    )(scalars, *operands)


def shape_of(shape, dtype):
    return jax.ShapeDtypeStruct(shape, dtype)


def project(me, pieces, square, gain, weight, kernel, masks):
    count = len(pieces)
    row_count = pieces[0].shape[0]
    full, part = weight.shape[0], kernel.shape[1]
    share = full // (4 if square else 1)
    packed = pl.BlockSpec((full, 3 * part), lambda *_: (0, 0), pipeline_mode=pl.Buffered(1))

    def body(me_ref, *refs):
        xs, (gain_ref, w_ref, k_ref, m_ref), (n_ref, x_ref, p_ref, v_ref, y_ref, s_ref), (carry,) = (
            refs[:count],
            refs[count : count + 4],
            refs[count + 4 : count + 10],
            refs[count + 10 :],
        )

        @pl.when(pl.program_id(0) == 0)
        def _():
            carry[...] = jnp.zeros_like(carry)

        values = [ref[...].astype(F32) for ref in xs]
        total = functools.reduce(jnp.add, [jnp.sum(v * v, axis=1, keepdims=True) for v in values])
        scale = lax.rsqrt(total / full + EPSILON)
        s_ref[...] = scale
        for ref, v, start in zip(xs, values, piece_starts(me_ref[0], share, square)):
            at = pl.ds(pl.multiple_of(start, 128), v.shape[1])
            n_ref[:, at] = (v * scale * gain_ref[:, at]).astype(BF)
            x_ref[:, at] = ref[...]
        mixed = jnp.dot(n_ref[...], w_ref[...], preferred_element_type=F32)
        p_ref[...] = mixed
        gated = mixed[:, :part] * mixed[:, 2 * part :]
        row = lax.broadcasted_iota(jnp.int32, gated.shape, 0)
        before, last = carry[6:7, :], carry[7:8, :]
        back_one = jnp.where(row == 0, last, pltpu.roll(gated, 1, 0))
        back_two = jnp.where(row == 0, before, jnp.where(row == 1, last, pltpu.roll(gated, 2, 0)))
        carry[...] = gated[-8:, :]
        keep = m_ref[...]
        filtered = (
            k_ref[0:1, :] * gated + k_ref[1:2, :] * keep[:, 0:1] * back_one + k_ref[2:3, :] * keep[:, 1:2] * back_two
        )
        v_ref[...] = filtered
        y_ref[...] = (mixed[:, part : 2 * part] * filtered).astype(BF)

    return run(
        body,
        (row_count // TILE,),
        me,
        [*pieces, gain, weight, kernel, masks],
        [tiles(p.shape[1]) for p in pieces] + [whole(gain.shape), packed, whole(kernel.shape), tiles(2)],
        [
            shape_of((row_count, full), BF),
            shape_of((row_count, full), BF),
            shape_of((row_count, 3 * part), F32),
            shape_of((row_count, part), F32),
            shape_of((row_count, part), BF),
            shape_of((row_count, 1), F32),
        ],
        [tiles(full), tiles(full), tiles(3 * part), tiles(part), tiles(part), tiles(1)],
        [pltpu.VMEM((8, part), F32)],
        flops=2 * row_count * full * 3 * part,
    )


def mix(core, pieces, mine, other, x_full, gain):
    count = len(pieces)
    row_count, full = x_full.shape
    packed = bool(other)
    mats = [*mine, *other]
    parts = len(mats)
    slab = pieces[0].shape[1] // 2

    def body(core_ref, *refs):
        ys, ms, (x_ref, gain_ref), (h_ref, n_ref, s_ref), (all_ref, *weight) = (
            refs[:count],
            refs[count : count + parts],
            refs[count + parts : count + parts + 2],
            refs[count + parts + 2 : count + parts + 5],
            refs[count + parts + 5 :],
        )
        weight_ref = weight[0] if packed else ms[0]

        if packed:

            @pl.when(pl.program_id(0) == 0)
            def _():
                for side in range(2):
                    start = (core_ref[0] ^ side) * (full // 2)
                    for k in range(5):
                        ref = ms[5 * side + k]
                        for n in range(ref.shape[0] // slab):
                            column = start + (n + (k == 4) * (full // 4 // slab)) * slab
                            at = pl.ds(pl.multiple_of(column, 128), slab)
                            for half in range(2):
                                row = (2 * min(k, 3) + half) * slab
                                weight_ref[row : row + slab, at] = ref[
                                    n * slab : (n + 1) * slab, half * slab : (half + 1) * slab
                                ]

        at = 0
        for ref in ys:
            all_ref[:, at : at + ref.shape[1]] = ref[...]
            at += ref.shape[1]
        h = x_ref[...].astype(F32) + jnp.dot(all_ref[...], weight_ref[...], preferred_element_type=F32)
        h_ref[...] = h
        scale = lax.rsqrt(jnp.sum(h * h, axis=1, keepdims=True) / full + EPSILON)
        s_ref[...] = scale
        n_ref[...] = (h * scale * gain_ref[...]).astype(BF)

    return run(
        body,
        (row_count // BIG,),
        core,
        [*pieces, *mats, x_full, gain],
        [tiles(p.shape[1], BIG) for p in pieces] + [whole(m.shape) for m in mats] + [tiles(full, BIG), whole(gain.shape)],
        [shape_of((row_count, full), F32), shape_of((row_count, full), BF), shape_of((row_count, 1), F32)],
        [tiles(full, BIG), tiles(full, BIG), tiles(1, BIG)],
        [pltpu.VMEM((BIG, full), BF)] + ([pltpu.VMEM((full, full), BF)] if packed else []),
        flops=2 * row_count * full * full,
    )


def lay(me, pieces, square):
    if not square:
        return pieces[0]
    row_count, share = pieces[0].shape
    full = 4 * share

    def body(me_ref, *refs):
        starts = piece_starts(me_ref[0], share, True)
        starts[4] = starts[3] + pieces[3].shape[1]
        for ref, start in zip(refs[:-1], starts):
            refs[-1][:, pl.ds(pl.multiple_of(start, 128), ref.shape[1])] = ref[...]

    return run(
        body,
        (row_count // BIG,),
        me,
        pieces,
        [tiles(p.shape[1], BIG) for p in pieces],
        [shape_of((row_count, full), BF)],
        [tiles(full, BIG)],
    )[0]


def expand(me, normed, weight):
    row_count, full = normed.shape
    units = weight.shape[1] // 2

    def body(_, n_ref, w_ref, q_ref, a_ref, b_ref):
        step = min(512, units)
        for at in range(0, units, step):
            gate = jnp.dot(n_ref[...], w_ref[:, at : at + step], preferred_element_type=F32)
            up = jnp.dot(n_ref[...], w_ref[:, units + at : units + at + step], preferred_element_type=F32)
            sig = 1.0 / (1.0 + jnp.exp(-gate))
            active = gate * sig
            q_ref[:, at : at + step] = (active * up).astype(BF)
            a_ref[:, at : at + step] = active.astype(BF)
            b_ref[:, at : at + step] = (up * sig * (1.0 + gate * (1.0 - sig))).astype(BF)

    return run(
        body,
        (row_count // BIG,),
        me,
        [normed, weight],
        [tiles(full, BIG), whole(weight.shape)],
        [shape_of((row_count, units), BF)] * 3,
        [tiles(units, BIG)] * 3,
        flops=2 * row_count * full * 2 * units,
    )


def ffn_back(owners, band, grad, slope_up, slope_gate, down, weight, d_both=None):
    bands = owners.shape[0]
    row_count, full = grad.shape
    units = down.shape[0]
    step = min(512, units)
    count = units // step

    def body(_, g_ref, a_ref, b_ref, d_ref, wg_ref, wu_ref, *refs):
        *halves_of, o_ref, total = refs[-2 * bands - 2 :]
        j = pl.program_id(1)
        dq = contract_cols(g_ref[...], d_ref[...])
        d_gate = (dq * b_ref[...].astype(F32)).astype(BF)
        d_up = (dq * a_ref[...].astype(F32)).astype(BF)
        at = pl.multiple_of(j * step, 128)
        o_ref[:, pl.ds(at, step)] = d_gate
        o_ref[:, pl.ds(units + at, step)] = d_up
        term = contract_cols(d_gate, wg_ref[...]) + contract_cols(d_up, wu_ref[...])

        @pl.when(j == 0)
        def _():
            total[...] = term

        @pl.when(j > 0)
        def _():
            total[...] += term

        for k in range(bands):

            @pl.when((pl.program_id(0) == k) & (j == count - 1))
            def _(k=k):
                halves_of[2 * k][...] = total[:, : full // 2].astype(BF)
                halves_of[2 * k + 1][...] = total[:, full // 2 :].astype(BF)

    return run(
        body,
        (bands, count),
        owners,
        [grad, slope_up, slope_gate, down, weight, weight] + ([] if d_both is None else [d_both]),
        [
            pl.BlockSpec((band, full), lambda i, j, o: (o[i], 0)),
            pl.BlockSpec((band, step), lambda i, j, o: (o[i], j)),
            pl.BlockSpec((band, step), lambda i, j, o: (o[i], j)),
            pl.BlockSpec((step, full), lambda i, j, o: (j, 0)),
            pl.BlockSpec((full, step), lambda i, j, o: (0, j)),
            pl.BlockSpec((full, step), lambda i, j, o: (0, count + j)),
        ]
        + ([] if d_both is None else [pl.BlockSpec(memory_space=pl.ANY)]),
        [shape_of((band, full // 2), BF)] * (2 * bands) + [shape_of((row_count, 2 * units), BF)],
        [pl.BlockSpec((band, full // 2), lambda i, j, o: (0, 0))] * (2 * bands)
        + [pl.BlockSpec((band, 2 * units), lambda i, j, o: (o[i], 0))],
        [pltpu.VMEM((band, full), F32)],
        flops=6 * bands * band * full * units,
        aliases=None if d_both is None else {7: 2 * bands},
    )


def hidden_back(me, terms, hidden, scale_two, grad, gain):
    band = terms[0][0].shape[0]
    full = gain.shape[1]
    tile = min(128, band)
    count = 2 * len(terms)

    def body(_, *refs):
        h_ref, s_ref, g_ref, gain_ref, o_ref, n_ref = refs[count:]

        @pl.when(pl.program_id(0) == 0)
        def _():
            n_ref[...] = jnp.zeros_like(n_ref)

        sums = [functools.reduce(jnp.add, [r[...].astype(F32) for r in refs[k:count:2]]) for k in (0, 1)]
        d_normed = jnp.concatenate(sums, axis=1)
        h, scale = h_ref[...], s_ref[...]
        scaled = d_normed * gain_ref[...]
        inner = jnp.sum(scaled * h, axis=1, keepdims=True) / full
        o_ref[...] = (g_ref[...].astype(F32) + scale * (scaled - h * scale * scale * inner)).astype(BF)
        n_ref[...] += jnp.sum(d_normed * h * scale, axis=0, keepdims=True)

    def mine(width):
        return pl.BlockSpec((tile, width), lambda i, o: (o[0] * (band // tile) + i, 0))

    flat = [half for pair in terms for half in pair]
    return run(
        body,
        (band // tile,),
        me,
        [*flat, hidden, scale_two, grad, gain],
        [tiles(f.shape[1], tile) for f in flat] + [mine(full), mine(1), mine(full), whole(gain.shape)],
        [shape_of((band, full), BF), shape_of((1, full), F32)],
        [tiles(full, tile), pl.BlockSpec((1, full), lambda i, *_: (0, 0))],
    )


def mixer_back(owners, pieces, out_rows, mixed, filtered, kernel, masks, weight):
    part, full = out_rows.shape
    row_count = mixed.shape[0]
    count = row_count // TILE
    size = owners.shape[0]
    given = len(pieces)
    assert given == 1 or row_count == size * TILE
    packed = pl.BlockSpec((full, 3 * part), lambda *_: (0, 0), pipeline_mode=pl.Buffered(1))

    def body(own_ref, *refs):
        w_ref, p_ref, v_ref, k_ref, m_ref, r_ref = refs[given : given + 6]
        outs = refs[given + 6 : given + 6 + 2 * size]
        o_ref, kg_ref, d_ref, carry, dy_ref = refs[given + 6 + 2 * size :]
        i = pl.program_id(0)

        @pl.when(i == 0)
        def _():
            carry[...] = jnp.zeros_like(carry)
            kg_ref[...] = jnp.zeros_like(kg_ref)

        first = (count - 1 - i) * TILE
        if given == 1:
            d_ref[...] = refs[0][pl.ds(pl.multiple_of(first, TILE), TILE), :]
        else:
            apart = (count - 1 - i) ^ own_ref[size - 1]
            for k in range(3):

                @pl.when(apart == k)
                def _(k=k):
                    d_ref[...] = refs[k][...]

            @pl.when(apart == 3)
            def _():
                d_ref[: TILE // 2, :] = refs[3][...]
                d_ref[TILE // 2 :, :] = refs[4][...]

        dy_ref[...] = contract_cols(d_ref[...], w_ref[...])
        dy = dy_ref[...]
        b, c, x = p_ref[:, :part], p_ref[:, part : 2 * part], p_ref[:, 2 * part :]
        dv = dy * c
        keep = m_ref[...]
        one, two = dv * keep[:, 0:1], dv * keep[:, 1:2]
        row = lax.broadcasted_iota(jnp.int32, dv.shape, 0)
        end = TILE - 1
        next_one = jnp.where(row == end, carry[0:1, :], pltpu.roll(one, TILE - 1, 0))
        next_two = jnp.where(
            row == end, carry[2:3, :], jnp.where(row == end - 1, carry[1:2, :], pltpu.roll(two, TILE - 2, 0))
        )
        carry[0:1, :] = one[0:1, :]
        carry[1:3, :] = two[0:2, :]
        u = b * x
        kg_ref[0:1, :] += jnp.sum(dv * u, axis=0, keepdims=True)
        kg_ref[1:2, :] += jnp.sum(next_one * u, axis=0, keepdims=True)
        kg_ref[2:3, :] += jnp.sum(next_two * u, axis=0, keepdims=True)
        du = k_ref[0:1, :] * dv + k_ref[1:2, :] * next_one + k_ref[2:3, :] * next_two
        o_ref[:, :part] = (du * x).astype(BF)
        o_ref[:, part : 2 * part] = (dy * v_ref[...]).astype(BF)
        o_ref[:, 2 * part :] = (du * b).astype(BF)
        for k in range(size):
            rows = pl.ds(pl.multiple_of(own_ref[k] * part, part), part)
            term = contract_cols(o_ref[...], r_ref[rows, :])
            outs[2 * k][...] = term[:, : part // 2].astype(BF)
            outs[2 * k + 1][...] = term[:, part // 2 :].astype(BF)

    def back(width):
        return pl.BlockSpec((TILE, width), lambda i, *_: (count - 1 - i, 0))

    return run(
        body,
        (count,),
        owners,
        [*pieces, out_rows, mixed, filtered, kernel, masks, weight],
        [whole(p.shape) for p in pieces]
        + [whole(out_rows.shape), back(3 * part), back(part), whole(kernel.shape), back(2), packed],
        [shape_of((row_count, part // 2), BF)] * (2 * size)
        + [shape_of((row_count, 3 * part), BF), shape_of((CONV, part), F32), shape_of((row_count, full), BF)],
        [back(part // 2)] * (2 * size)
        + [back(3 * part), pl.BlockSpec((CONV, part), lambda i, *_: (0, 0)), back(full)],
        [pltpu.VMEM((8, part), F32), pltpu.VMEM((TILE, part), F32)],
        flops=2 * row_count * full * part * 4,
    )


def front_terms(owners, left, right):
    row_count, depth = left.shape
    size = owners.shape[0]
    width = right.shape[1] // size

    def body(own_ref, l_ref, r_ref, *outs):
        for k in range(size):
            at = pl.ds(pl.multiple_of(own_ref[k] * width, width), width)
            term = jnp.dot(l_ref[...], r_ref[:, at], preferred_element_type=F32)
            outs[2 * k][...] = term[:, : width // 2].astype(BF)
            outs[2 * k + 1][...] = term[:, width // 2 :].astype(BF)

    return run(
        body,
        (row_count // BIG,),
        owners,
        [left, right],
        [tiles(depth, BIG), whole(right.shape)],
        [shape_of((row_count, width // 2), BF)] * (2 * size),
        [tiles(width // 2, BIG)] * (2 * size),
        flops=2 * row_count * depth * width * size,
    )


def add_low(left, right):
    return (left.astype(F32) + right.astype(F32)).astype(BF)


def scatter_plain(terms, axis):
    joined = jnp.concatenate([jnp.concatenate(pair, axis=1) for pair in terms], axis=axis).astype(F32)
    return lax.psum_scatter(joined, "narrow", scatter_dimension=axis, tiled=True)


def total_of(pairs):
    return jnp.concatenate(
        [functools.reduce(jnp.add, [pair[k].astype(F32) for pair in pairs]) for k in (0, 1)], axis=1
    )


def wide_all(block, axis):
    return lax.all_gather(block, "wide", axis=axis, tiled=True)


def wide_sums(terms, axis):
    return lax.psum_scatter(terms.astype(BF), "wide", scatter_dimension=axis, tiled=True)


def narrow_total(values, square):
    if not square:
        return lax.psum(values, "narrow")
    values = values + to_x(values)
    return values + to_y(values)


def wide_total(values, square):
    if not square:
        return lax.psum(values, "wide")
    for bit in (1, 2, 4):
        values = values + lax.ppermute(values, "wide", [(i, i ^ bit) for i in range(lax.axis_size("wide"))])
    return values


def to_core(values):
    return lax.ppermute(values, "wide", [(i, i ^ 1) for i in range(lax.axis_size("wide"))])


def line_step(state, step):
    sums, right, left = state
    z = lax.axis_index("wide") // 2

    def with_own(come, chip):
        own = lax.dynamic_index_in_dim(sums, jnp.clip(chip, 0, 3), 0, keepdims=False)
        return own if come is None else add_low(own, come)

    return (
        sums,
        lax.ppermute(with_own(right, z + 4 - step), "wide", [(w, w + 2) for w in range(2 * step)]),
        lax.ppermute(with_own(left, z - 4 + step), "wide", [(w, w - 2) for w in range(8 - 2 * step, 8)]),
    )


def line_start(terms, core):
    blocks = terms.reshape(4, 2, terms.shape[0] // 8, terms.shape[1])
    other = to_core(lax.dynamic_index_in_dim(blocks, 1 - core, 1, keepdims=False))
    sums = add_low(lax.dynamic_index_in_dim(blocks, core, 1, keepdims=False), other)
    return line_step((sums, None, None), 1)


def line_end(state):
    sums, right, left = line_step(state, 3)
    own = lax.dynamic_index_in_dim(sums, lax.axis_index("wide") // 2, 0, keepdims=False)
    return own.astype(F32) + right.astype(F32) + left.astype(F32)


def after(value, *others):
    return lax.optimization_barrier((value, *others))[0]


def per_device(
    square,
    size,
    tokens,
    segment_ids,
    norm1_gain,
    in_weight,
    conv_weight,
    out_weight,
    norm2_gain,
    gate_weight,
    up_weight,
    down_weight,
    cotangent,
):
    full_width = norm1_gain.shape[0]
    part_width = tokens.shape[1]
    units = gate_weight.shape[1]
    row_count = tokens.shape[0]
    band = row_count // size
    me = lax.axis_index("narrow")
    core = lax.axis_index("wide") % 2
    me_s = me.reshape(1).astype(jnp.int32)
    core_s = core.reshape(1).astype(jnp.int32)
    offset = me * part_width
    kernel = lax.dynamic_slice_in_dim(conv_weight, offset, part_width, 1)
    gain_one, gain_two = norm1_gain[None, :], norm2_gain[None, :]

    order = [me ^ 3, me ^ 1, me ^ 2, me] if square else list(range(size))
    owners = jnp.stack([jnp.asarray(o, jnp.int32) for o in order])

    positions = lax.broadcasted_iota(jnp.int32, (row_count,), 0)
    masks = jnp.stack(
        [((positions >= k) & (segment_ids == lagged(segment_ids, k))).astype(F32) for k in (1, 2)], axis=1
    )
    barrier = lax.optimization_barrier
    in_cols = 3 * part_width
    pack = [in_weight[:, k] for k in range(3)]
    both = jnp.concatenate([gate_weight, up_weight], axis=1)

    def project_rows(x_pieces, in_all):
        return tuple(project(me_s, x_pieces, square, gain_one, in_all, kernel, masks))

    def unpacked(in_all):
        rows = in_all[:, in_cols:].reshape(-1, pack[0].shape[0], 2, part_width // 2)
        return rows.transpose(2, 1, 0, 3).reshape(part_width, full_width)

    if square:
        in_all = wide_all(jnp.concatenate(pack + list(halves(out_weight, 0)), axis=1), 0)
        x_pieces = gather_pieces(tokens, 1, True)[0]
        both_all = wide_all(after(both, *x_pieces), 0)

        half_cols = full_width // 2
        own_out = lax.dynamic_slice(in_all, (core * half_cols, jnp.int32(in_cols)), (half_cols, part_width))
        low_grad, high_grad = cotangent[:, : part_width // 4], cotangent[:, part_width // 4 :]
        x_out, y_out, low_far, projected = barrier(
            (to_x(own_out), to_y(own_out), to_far(after(low_grad, *x_pieces)), project_rows(x_pieces, in_all))
        )
        normed_one, x_full, mixed, filtered, mixer_low, scale_one = projected
        down_all = wide_all(after(down_weight, mixer_low), 1)
        x_mix, y_mix = barrier((to_x(mixer_low), to_y(mixer_low)))
        low_out, high_out = to_x(halves(y_out, 0)[0]), to_y(halves(x_out, 0)[1])
        low_mix, high_mix, low_out, high_out, *near = barrier(
            (
                to_x(halves(y_mix, 1)[0]),
                to_y(halves(x_mix, 1)[1]),
                low_out,
                high_out,
                to_core(own_out),
                to_core(x_out),
                to_core(y_out),
            )
        )
        far = [to_core(low_out), to_core(high_out)]
        y_pieces = [mixer_low, x_mix, y_mix, low_mix, high_mix]
        mine, other = [own_out, x_out, y_out, low_out, high_out], [*near, *far]
        grad_now, high_now, _ = barrier((cotangent, high_grad, low_mix))
        hidden, normed_two, scale_two = mix(core_s, y_pieces, mine, other, x_full, gain_two)
        x_grad, y_grad, high_far, (hidden_low, slope_up, slope_gate) = barrier(
            (to_x(grad_now), to_y(grad_now), to_far(high_now), expand(me_s, normed_two, both_all))
        )
        g_pieces = [cotangent, x_grad, y_grad, low_far, high_far]
    else:
        in_all = wide_all(jnp.concatenate(pack, axis=1), 0)
        out_rows = wide_all(out_weight, 1)
        x_pieces = gather_pieces(tokens, 1, False)[0]
        both_all = wide_all(both, 0)
        down_all = wide_all(down_weight, 1)
        normed_one, x_full, mixed, filtered, mixer_low, scale_one = project_rows(x_pieces, in_all)
        y_pieces = gather_pieces(mixer_low, 1, False)[0]
        mine, other = [lax.all_gather(out_rows, "narrow", axis=0, tiled=True)], []
        hidden, normed_two, scale_two = mix(core_s, y_pieces, mine, other, x_full, gain_two)
        hidden_low, slope_up, slope_gate = expand(me_s, normed_two, both_all)
        g_pieces = gather_pieces(cotangent, 1, False)[0]
    grad_full = lay(me_s, g_pieces, square)
    down_terms = contract_rows(hidden_low, grad_full).astype(BF)
    down_grad = wide_sums(down_terms, 1)
    slope_up = after(slope_up, down_terms)

    def ffn(which, d_both):
        *parts, d_both = ffn_back(which, band, grad_full, slope_up, slope_gate, down_all, both_all, d_both)
        return list(zip(parts[0::2], parts[1::2])), d_both

    def mixer(dh_pieces, out_rows):
        *parts, d_flat, kernel_grad, d_hidden_low = mixer_back(
            owners, dh_pieces, out_rows, mixed, filtered, kernel, masks, in_all
        )
        return list(zip(parts[0::2], parts[1::2])), d_flat, kernel_grad, d_hidden_low

    def dh_of(sums):
        return hidden_back(me_s, sums, hidden, scale_two, grad_full, gain_two)

    def out_terms_of(hidden_low):
        parts = front_terms(owners, hidden_low, down_all)
        return list(zip(parts[0::2], parts[1::2]))

    if square:
        (across, for_x), d_both = ffn(owners[:2], None)
        via_x, via_y, ((for_y,), d_both) = barrier((to_x(across[0]), to_y(across[1]), ffn(owners[2:3], d_both)))
        x_low, y_high, x_high, y_low, ((own,), d_both) = barrier(
            (
                to_x(after(for_x[0], via_x)),
                to_y(for_y[1]),
                add_low(for_x[1], via_y),
                add_low(for_y[0], via_x),
                ffn(owners[3:], d_both),
            )
        )
        x_high, y_low, gate_terms = barrier(
            (to_x(x_high), to_y(y_low), contract_rows(normed_two, d_both[:, :units]).astype(BF))
        )
        gate_grad = wide_sums(gate_terms, 0)
        y_high = after(y_high, down_grad)
        d_hidden_rows, gain_two_terms = dh_of([own, (x_low, x_high), (y_low, y_high)])

        def beside_dh():
            up_terms = contract_rows(after(normed_two, d_hidden_rows), d_both[:, units:]).astype(BF)
            return up_terms, out_terms_of(after(hidden_low, up_terms)), unpacked(after(in_all, d_hidden_rows))

        dh_pieces, (up_terms, out_parts, out_rows), _ = gather_pieces(
            d_hidden_rows, 0, True, (beside_dh, lambda _: ())
        )
        up_grad = wide_sums(up_terms, 0)
        out_parts, gate_grad = barrier((out_parts, gate_grad))
        out_first = [tuple(after(half, *dh_pieces[3:]) for half in part) for part in out_parts]
        out_via_x, out_via_y, out_x_low, out_y_high, (one_parts, d_flat, kernel_grad, d_hidden_low) = barrier(
            (
                to_x(out_first[0][0]),
                to_y(out_first[0][1]),
                to_x(out_first[1][0]),
                to_y(out_first[2][1]),
                mixer(dh_pieces, out_rows),
            )
        )
        via_x, via_y, in_terms = barrier(
            (to_x(one_parts[0][0]), to_y(one_parts[0][1]), contract_rows(normed_one, d_flat).astype(BF))
        )
        x_low, y_high, x_high, y_low, out_x_high, out_y_low, out_terms, in_terms, up_grad = barrier(
            (
                to_x(after(one_parts[1][0], via_x)),
                to_y(after(one_parts[2][1], via_y)),
                add_low(one_parts[1][1], via_y),
                add_low(one_parts[2][0], via_x),
                add_low(out_parts[1][1], out_via_y),
                add_low(out_parts[2][0], out_via_x),
                contract_rows(after(d_hidden_low, in_terms), mixer_low).astype(BF),
                in_terms,
                up_grad,
            )
        )
        in_grad = wide_sums(in_terms, 0)
        x_high, y_low, line = barrier((to_x(x_high), to_y(y_low), line_start(out_terms, core)))
        d_normed_one = total_of([one_parts[3], (x_low, x_high), (y_low, y_high)])
        my_gain = lax.dynamic_slice_in_dim(norm1_gain, offset, part_width)
        inner_one = jnp.sum(d_normed_one * my_gain * tokens.astype(F32), axis=1).reshape(-1, 128)
        out_x_high, out_y_low, inner_one, line = barrier(
            (
                to_x(after(out_x_high, x_low, x_high)),
                to_y(after(out_y_low, y_low, y_high)),
                inner_one + to_x(inner_one),
                line_step(line, 2),
            )
        )
        inner_one = inner_one + to_y(inner_one)
        out_grad = line_end(line).T
        ffn_out = total_of([out_parts[3], (out_x_low, out_x_high), (out_y_low, out_y_high)])
    else:
        ffn_terms, d_both = ffn(owners, None)
        both_grad = wide_sums(contract_rows(normed_two, d_both), 0)
        gate_grad, up_grad = both_grad[:, :units], both_grad[:, units:]
        d_hidden_rows, gain_two_terms = dh_of([tuple(halves(scatter_plain(ffn_terms, 0), 1))])
        one_parts, d_flat, kernel_grad, d_hidden_low = mixer(gather_pieces(d_hidden_rows, 0, False)[0], out_rows)
        d_normed_one = scatter_plain(one_parts, 1)
        ffn_out = scatter_plain(out_terms_of(hidden_low), 1)
        in_grad = wide_sums(contract_rows(normed_one, d_flat), 0)
        out_grad = wide_sums(contract_rows(mixer_low, d_hidden_low), 1)
    in_grad = jnp.stack([in_grad[:, k * part_width : (k + 1) * part_width] for k in range(3)], axis=1)
    block_out = (lax.dynamic_slice_in_dim(hidden, offset, part_width, 1) + ffn_out).astype(BF)

    my_gain = lax.dynamic_slice_in_dim(norm1_gain, offset, part_width)
    x_part = tokens.astype(F32)
    scaled_one = d_normed_one * my_gain
    if not square:
        inner_one = lax.psum(jnp.sum(scaled_one * x_part, axis=1), "narrow")
    inner_one = inner_one.reshape(row_count, 1) / full_width
    tokens_grad = (
        lax.dynamic_slice_in_dim(d_hidden_low, offset, part_width, 1).astype(F32)
        + scale_one * (scaled_one - x_part * scale_one * scale_one * inner_one)
    ).astype(BF)
    gain_one_grad = jnp.sum(d_normed_one * x_part * scale_one, axis=0)
    gain_two_terms = narrow_total(after(gain_two_terms, ffn_out).reshape(size, part_width), square)
    gain_two_terms = lax.dynamic_slice_in_dim(gain_two_terms, me, 1, 0)
    small = wide_total(jnp.concatenate([gain_one_grad[None, :], gain_two_terms, kernel_grad], axis=0), square)
    gain_one_grad, gain_two_grad, kernel_grad = small[0], small[1], small[2:]
    return (
        block_out,
        tokens_grad,
        gain_one_grad,
        in_grad.astype(F32),
        kernel_grad,
        out_grad.astype(F32),
        gain_two_grad,
        gate_grad.astype(F32),
        up_grad.astype(F32),
        down_grad.astype(F32),
    )


def solution(mesh):
    size = mesh.shape["narrow"]
    square = size == 4 and mesh.shape["wide"] == 8

    def step(*args):
        return per_device(square, size, *args)

    in_specs = (
        P("wide", "narrow"),
        P("wide"),
        P(),
        P("wide", None, "narrow"),
        P(),
        P("narrow", "wide"),
        P(),
        P("wide", "narrow"),
        P("wide", "narrow"),
        P("narrow", "wide"),
        P("wide", "narrow"),
    )
    out_specs = (
        P("wide", "narrow"),
        P("wide", "narrow"),
        P("narrow"),
        P("wide", None, "narrow"),
        P(None, "narrow"),
        P("narrow", "wide"),
        P("narrow"),
        P("wide", "narrow"),
        P("wide", "narrow"),
        P("narrow", "wide"),
    )
    return jax.shard_map(step, mesh=mesh, in_specs=in_specs, out_specs=out_specs, check_vma=False)
```

```python
import functools

import jax
import jax.numpy as jnp
from jax import lax
from jax.experimental import pallas as pl
from jax.experimental.pallas import tpu as pltpu
from jax.sharding import PartitionSpec as P

CONV = 3
EPSILON = 1e-05
BF = jnp.bfloat16
F32 = jnp.float32
TILE = 512
BIG = 512


def contract_rows(left, right):
    return lax.dot_general(left, right, (((0,), (0,)), ((), ())), preferred_element_type=F32)


def contract_cols(left, right):
    return lax.dot_general(left, right, (((1,), (1,)), ((), ())), preferred_element_type=F32)


def lagged(values, shift_by):
    head = jnp.zeros((shift_by,) + values.shape[1:], values.dtype)
    return jnp.concatenate([head, values[: values.shape[0] - shift_by]], axis=0)


ALONG_X = [(0, 1), (1, 0), (2, 3), (3, 2)]
ALONG_Y = [(0, 2), (2, 0), (1, 3), (3, 1)]
ACROSS = [(0, 3), (3, 0), (1, 2), (2, 1)]


def to_x(values):
    return lax.ppermute(values, "narrow", ALONG_X)


def to_y(values):
    return lax.ppermute(values, "narrow", ALONG_Y)


def to_far(values):
    return lax.ppermute(values, "narrow", ACROSS)


def halves(values, axis):
    middle = values.shape[axis] // 2
    return lax.slice_in_dim(values, 0, middle, axis=axis), lax.slice_in_dim(values, middle, None, axis=axis)


def gather_pieces(block, axis, square, beside=(lambda: (), lambda _: ())):
    if not square:
        first = beside[0]()
        return [lax.all_gather(block, "narrow", axis=axis, tiled=True)], first, beside[1](first)
    from_x, from_y, first = lax.optimization_barrier((to_x(block), to_y(block), beside[0]()))
    low, high, second = lax.optimization_barrier(
        (to_x(halves(from_y, axis)[0]), to_y(halves(from_x, axis)[1]), beside[1](first))
    )
    return [block, from_x, from_y, low, high], first, second


def piece_starts(me, width, square):
    if not square:
        return [0]
    return [me * width, (me ^ 1) * width, (me ^ 2) * width, (me ^ 3) * width, (me ^ 3) * width + width // 2]


def whole(shape):
    return pl.BlockSpec(shape, lambda *_: (0,) * len(shape), pipeline_mode=pl.Buffered(1))


def tiles(width, tile=TILE):
    return pl.BlockSpec((tile, width), lambda i, *_: (i, 0))


def run(kernel, grid, scalars, operands, in_specs, outs, out_specs, scratch=(), flops=0, aliases=None, vmem=56):
    moved = sum(o.size * o.dtype.itemsize for o in operands) + sum(o.size * o.dtype.itemsize for o in outs)
    return pl.pallas_call(
        kernel,
        grid_spec=pltpu.PrefetchScalarGridSpec(
            num_scalar_prefetch=1, grid=grid, in_specs=in_specs, out_specs=out_specs, scratch_shapes=list(scratch)
        ),
        out_shape=outs,
        input_output_aliases=aliases or {},
        cost_estimate=pl.CostEstimate(flops=flops, bytes_accessed=moved, transcendentals=0),
        compiler_params=pltpu.CompilerParams(
            dimension_semantics=("arbitrary",) * len(grid), vmem_limit_bytes=vmem << 20
        ),
    )(scalars, *operands)


def shape_of(shape, dtype):
    return jax.ShapeDtypeStruct(shape, dtype)


def packed_block(in_parts, out_block):
    slim, part = in_parts.shape[1:]

    def body(_, in_ref, out_ref, o_ref):
        for k in range(3):
            o_ref[:, k * part : (k + 1) * part] = in_ref[k]
        for k in range(2):
            at = 3 * part + k * (part // 2)
            o_ref[:, at : at + part // 2] = out_ref[k * slim : (k + 1) * slim, :]

    return run(
        body,
        (1,),
        jnp.zeros((1,), jnp.int32),
        [in_parts, out_block],
        [whole(in_parts.shape), whole(out_block.shape)],
        [shape_of((slim, 4 * part), BF)],
        [whole((slim, 4 * part))],
        vmem=16,
    )[0]


def project(me, pieces, square, gain, weight, kernel, masks):
    count = len(pieces)
    row_count = pieces[0].shape[0]
    full, part = weight.shape[0], kernel.shape[1]
    share = full // (4 if square else 1)
    packed = pl.BlockSpec((full, 3 * part), lambda *_: (0, 0), pipeline_mode=pl.Buffered(1))

    def body(me_ref, *refs):
        xs, (gain_ref, w_ref, k_ref, m_ref), (n_ref, x_ref, p_ref, v_ref, y_ref, s_ref), (carry,) = (
            refs[:count],
            refs[count : count + 4],
            refs[count + 4 : count + 10],
            refs[count + 10 :],
        )

        @pl.when(pl.program_id(0) == 0)
        def _():
            carry[...] = jnp.zeros_like(carry)

        values = [ref[...].astype(F32) for ref in xs]
        total = functools.reduce(jnp.add, [jnp.sum(v * v, axis=1, keepdims=True) for v in values])
        scale = lax.rsqrt(total / full + EPSILON)
        s_ref[...] = scale
        for ref, v, start in zip(xs, values, piece_starts(me_ref[0], share, square)):
            at = pl.ds(pl.multiple_of(start, 128), v.shape[1])
            n_ref[:, at] = (v * scale * gain_ref[:, at]).astype(BF)
            x_ref[:, at] = ref[...]
        mixed = jnp.dot(n_ref[...], w_ref[...], preferred_element_type=F32)
        p_ref[...] = mixed
        gated = mixed[:, :part] * mixed[:, 2 * part :]
        row = lax.broadcasted_iota(jnp.int32, gated.shape, 0)
        before, last = carry[6:7, :], carry[7:8, :]
        back_one = jnp.where(row == 0, last, pltpu.roll(gated, 1, 0))
        back_two = jnp.where(row == 0, before, jnp.where(row == 1, last, pltpu.roll(gated, 2, 0)))
        carry[...] = gated[-8:, :]
        keep = m_ref[...]
        filtered = (
            k_ref[0:1, :] * gated + k_ref[1:2, :] * keep[:, 0:1] * back_one + k_ref[2:3, :] * keep[:, 1:2] * back_two
        )
        v_ref[...] = filtered
        y_ref[...] = (mixed[:, part : 2 * part] * filtered).astype(BF)

    return run(
        body,
        (row_count // TILE,),
        me,
        [*pieces, gain, weight, kernel, masks],
        [tiles(p.shape[1]) for p in pieces] + [whole(gain.shape), packed, whole(kernel.shape), tiles(2)],
        [
            shape_of((row_count, full), BF),
            shape_of((row_count, full), BF),
            shape_of((row_count, 3 * part), F32),
            shape_of((row_count, part), F32),
            shape_of((row_count, part), BF),
            shape_of((row_count, 1), F32),
        ],
        [tiles(full), tiles(full), tiles(3 * part), tiles(part), tiles(part), tiles(1)],
        [pltpu.VMEM((8, part), F32)],
        flops=2 * row_count * full * 3 * part,
    )


def mix(core, pieces, mine, other, x_full, gain):
    count = len(pieces)
    row_count, full = x_full.shape
    packed = bool(other)
    mats = [*mine, *other]
    parts = len(mats)
    slab = pieces[0].shape[1] // 2

    def body(core_ref, *refs):
        ys, ms, (x_ref, gain_ref), (h_ref, n_ref, s_ref), (all_ref, *weight) = (
            refs[:count],
            refs[count : count + parts],
            refs[count + parts : count + parts + 2],
            refs[count + parts + 2 : count + parts + 5],
            refs[count + parts + 5 :],
        )
        weight_ref = weight[0] if packed else ms[0]

        if packed:

            @pl.when(pl.program_id(0) == 0)
            def _():
                for side in range(2):
                    start = (core_ref[0] ^ side) * (full // 2)
                    for k in range(5):
                        ref = ms[5 * side + k]
                        for n in range(ref.shape[0] // slab):
                            column = start + (n + (k == 4) * (full // 4 // slab)) * slab
                            at = pl.ds(pl.multiple_of(column, 128), slab)
                            for half in range(2):
                                row = (2 * min(k, 3) + half) * slab
                                weight_ref[row : row + slab, at] = ref[
                                    n * slab : (n + 1) * slab, half * slab : (half + 1) * slab
                                ]

        at = 0
        for ref in ys:
            all_ref[:, at : at + ref.shape[1]] = ref[...]
            at += ref.shape[1]
        h = x_ref[...].astype(F32) + jnp.dot(all_ref[...], weight_ref[...], preferred_element_type=F32)
        h_ref[...] = h
        scale = lax.rsqrt(jnp.sum(h * h, axis=1, keepdims=True) / full + EPSILON)
        s_ref[...] = scale
        n_ref[...] = (h * scale * gain_ref[...]).astype(BF)

    return run(
        body,
        (row_count // BIG,),
        core,
        [*pieces, *mats, x_full, gain],
        [tiles(p.shape[1], BIG) for p in pieces] + [whole(m.shape) for m in mats] + [tiles(full, BIG), whole(gain.shape)],
        [shape_of((row_count, full), F32), shape_of((row_count, full), BF), shape_of((row_count, 1), F32)],
        [tiles(full, BIG), tiles(full, BIG), tiles(1, BIG)],
        [pltpu.VMEM((BIG, full), BF)] + ([pltpu.VMEM((full, full), BF)] if packed else []),
        flops=2 * row_count * full * full,
    )


def lay(me, pieces, square):
    if not square:
        return pieces[0]
    row_count, share = pieces[0].shape
    full = 4 * share

    def body(me_ref, *refs):
        starts = piece_starts(me_ref[0], share, True)
        starts[4] = starts[3] + pieces[3].shape[1]
        for ref, start in zip(refs[:-1], starts):
            refs[-1][:, pl.ds(pl.multiple_of(start, 128), ref.shape[1])] = ref[...]

    return run(
        body,
        (row_count // BIG,),
        me,
        pieces,
        [tiles(p.shape[1], BIG) for p in pieces],
        [shape_of((row_count, full), BF)],
        [tiles(full, BIG)],
    )[0]


def expand(me, normed, weight):
    row_count, full = normed.shape
    units = weight.shape[1] // 2

    def body(_, n_ref, w_ref, q_ref, a_ref, b_ref):
        step = min(512, units)
        for at in range(0, units, step):
            gate = jnp.dot(n_ref[...], w_ref[:, at : at + step], preferred_element_type=F32)
            up = jnp.dot(n_ref[...], w_ref[:, units + at : units + at + step], preferred_element_type=F32)
            sig = 1.0 / (1.0 + jnp.exp(-gate))
            active = gate * sig
            q_ref[:, at : at + step] = (active * up).astype(BF)
            a_ref[:, at : at + step] = active.astype(BF)
            b_ref[:, at : at + step] = (up * sig * (1.0 + gate * (1.0 - sig))).astype(BF)

    return run(
        body,
        (row_count // BIG,),
        me,
        [normed, weight],
        [tiles(full, BIG), whole(weight.shape)],
        [shape_of((row_count, units), BF)] * 3,
        [tiles(units, BIG)] * 3,
        flops=2 * row_count * full * 2 * units,
    )


def ffn_back(owners, band, grad, slope_up, slope_gate, down, weight, d_both=None):
    bands = owners.shape[0]
    row_count, full = grad.shape
    units = down.shape[0]
    step = min(512, units)
    count = units // step

    def body(_, g_ref, a_ref, b_ref, d_ref, wg_ref, wu_ref, *refs):
        *halves_of, dg_ref, du_ref, total = refs[-2 * bands - 3 :]
        j = pl.program_id(1)
        dq = contract_cols(g_ref[...], d_ref[...])
        d_gate = (dq * b_ref[...].astype(F32)).astype(BF)
        d_up = (dq * a_ref[...].astype(F32)).astype(BF)
        dg_ref[...] = d_gate
        du_ref[...] = d_up
        term = contract_cols(d_gate, wg_ref[...]) + contract_cols(d_up, wu_ref[...])

        @pl.when(j == 0)
        def _():
            total[...] = term

        @pl.when(j > 0)
        def _():
            total[...] += term

        for k in range(bands):

            @pl.when((pl.program_id(0) == k) & (j == count - 1))
            def _(k=k):
                halves_of[2 * k][...] = total[:, : full // 2].astype(BF)
                halves_of[2 * k + 1][...] = total[:, full // 2 :].astype(BF)

    return run(
        body,
        (bands, count),
        owners,
        [grad, slope_up, slope_gate, down, weight, weight] + list(d_both or []),
        [
            pl.BlockSpec((band, full), lambda i, j, o: (o[i], 0)),
            pl.BlockSpec((band, step), lambda i, j, o: (o[i], j)),
            pl.BlockSpec((band, step), lambda i, j, o: (o[i], j)),
            pl.BlockSpec((step, full), lambda i, j, o: (j, 0)),
            pl.BlockSpec((full, step), lambda i, j, o: (0, j)),
            pl.BlockSpec((full, step), lambda i, j, o: (0, count + j)),
        ]
        + [pl.BlockSpec(memory_space=pl.ANY)] * len(d_both or []),
        [shape_of((band, full // 2), BF)] * (2 * bands) + [shape_of((row_count, units), BF)] * 2,
        [pl.BlockSpec((band, full // 2), lambda i, j, o: (0, 0))] * (2 * bands)
        + [pl.BlockSpec((band, step), lambda i, j, o: (o[i], j))] * 2,
        [pltpu.VMEM((band, full), F32)],
        flops=6 * bands * band * full * units,
        aliases={7: 2 * bands, 8: 2 * bands + 1} if d_both else None,
    )


def hidden_back(me, terms, hidden, scale_two, grad, gain):
    band = terms[0][0].shape[0]
    full = gain.shape[1]
    tile = min(128, band)
    count = 2 * len(terms)

    def body(_, *refs):
        h_ref, s_ref, g_ref, gain_ref, o_ref, n_ref = refs[count:]

        @pl.when(pl.program_id(0) == 0)
        def _():
            n_ref[...] = jnp.zeros_like(n_ref)

        sums = [functools.reduce(jnp.add, [r[...].astype(F32) for r in refs[k:count:2]]) for k in (0, 1)]
        d_normed = jnp.concatenate(sums, axis=1)
        h, scale = h_ref[...], s_ref[...]
        scaled = d_normed * gain_ref[...]
        inner = jnp.sum(scaled * h, axis=1, keepdims=True) / full
        o_ref[...] = (g_ref[...].astype(F32) + scale * (scaled - h * scale * scale * inner)).astype(BF)
        n_ref[...] += jnp.sum(d_normed * h * scale, axis=0, keepdims=True)

    def mine(width):
        return pl.BlockSpec((tile, width), lambda i, o: (o[0] * (band // tile) + i, 0))

    flat = [half for pair in terms for half in pair]
    return run(
        body,
        (band // tile,),
        me,
        [*flat, hidden, scale_two, grad, gain],
        [tiles(f.shape[1], tile) for f in flat] + [mine(full), mine(1), mine(full), whole(gain.shape)],
        [shape_of((band, full), BF), shape_of((1, full), F32)],
        [tiles(full, tile), pl.BlockSpec((1, full), lambda i, *_: (0, 0))],
    )


def mixer_back(owners, pieces, out_rows, mixed, filtered, kernel, masks, weight, x_full, scale_one, gain):
    part, full = out_rows.shape
    row_count = mixed.shape[0]
    count = row_count // TILE
    size = owners.shape[0]
    given = len(pieces)
    assert given == 1 or row_count == size * TILE
    packed = pl.BlockSpec((full, 3 * part), lambda *_: (0, 0), pipeline_mode=pl.Buffered(1))

    def body(own_ref, *refs):
        w_ref, p_ref, v_ref, k_ref, m_ref, r_ref, x_ref, s_ref, gain_ref = refs[given : given + 9]
        outs = refs[given + 9 : given + 9 + 2 * size]
        o_ref, kg_ref, d_ref, row_ref, g_ref, carry, dy_ref = refs[given + 9 + 2 * size :]
        i = pl.program_id(0)

        @pl.when(i == 0)
        def _():
            carry[...] = jnp.zeros_like(carry)
            kg_ref[...] = jnp.zeros_like(kg_ref)
            g_ref[...] = jnp.zeros_like(g_ref)

        first = (count - 1 - i) * TILE
        if given == 1:
            d_ref[...] = refs[0][pl.ds(pl.multiple_of(first, TILE), TILE), :]
        else:
            apart = (count - 1 - i) ^ own_ref[size - 1]
            for k in range(3):

                @pl.when(apart == k)
                def _(k=k):
                    d_ref[...] = refs[k][...]

            @pl.when(apart == 3)
            def _():
                d_ref[: TILE // 2, :] = refs[3][...]
                d_ref[TILE // 2 :, :] = refs[4][...]

        dy_ref[...] = contract_cols(d_ref[...], w_ref[...])
        dy = dy_ref[...]
        b, c, x = p_ref[:, :part], p_ref[:, part : 2 * part], p_ref[:, 2 * part :]
        dv = dy * c
        keep = m_ref[...]
        one, two = dv * keep[:, 0:1], dv * keep[:, 1:2]
        row = lax.broadcasted_iota(jnp.int32, dv.shape, 0)
        end = TILE - 1
        next_one = jnp.where(row == end, carry[0:1, :], pltpu.roll(one, TILE - 1, 0))
        next_two = jnp.where(
            row == end, carry[2:3, :], jnp.where(row == end - 1, carry[1:2, :], pltpu.roll(two, TILE - 2, 0))
        )
        carry[0:1, :] = one[0:1, :]
        carry[1:3, :] = two[0:2, :]
        u = b * x
        kg_ref[0:1, :] += jnp.sum(dv * u, axis=0, keepdims=True)
        kg_ref[1:2, :] += jnp.sum(next_one * u, axis=0, keepdims=True)
        kg_ref[2:3, :] += jnp.sum(next_two * u, axis=0, keepdims=True)
        du = k_ref[0:1, :] * dv + k_ref[1:2, :] * next_one + k_ref[2:3, :] * next_two
        o_ref[:, :part] = (du * x).astype(BF)
        o_ref[:, part : 2 * part] = (dy * v_ref[...]).astype(BF)
        o_ref[:, 2 * part :] = (du * b).astype(BF)
        total = 0.0
        for k in range(size):
            rows = pl.ds(pl.multiple_of(own_ref[k] * part, part), part)
            term = contract_cols(o_ref[...], r_ref[rows, :])
            by_x = term * x_ref[:, rows].astype(F32)
            total = total + jnp.sum(by_x * gain_ref[:, rows], axis=1, keepdims=True)
            g_ref[:, rows] += jnp.sum(by_x * s_ref[...], axis=0, keepdims=True)
            outs[2 * k][...] = term[:, : part // 2].astype(BF)
            outs[2 * k + 1][...] = term[:, part // 2 :].astype(BF)
        row_ref[...] = total

    def back(width):
        return pl.BlockSpec((TILE, width), lambda i, *_: (count - 1 - i, 0))

    return run(
        body,
        (count,),
        owners,
        [*pieces, out_rows, mixed, filtered, kernel, masks, weight, x_full, scale_one, gain],
        [whole(p.shape) for p in pieces]
        + [whole(out_rows.shape), back(3 * part), back(part), whole(kernel.shape), back(2), packed]
        + [back(full), back(1), whole(gain.shape)],
        [shape_of((row_count, part // 2), BF)] * (2 * size)
        + [shape_of((row_count, 3 * part), BF), shape_of((CONV, part), F32), shape_of((row_count, full), BF)]
        + [shape_of((row_count, 1), F32), shape_of((1, full), F32)],
        [back(part // 2)] * (2 * size)
        + [back(3 * part), pl.BlockSpec((CONV, part), lambda i, *_: (0, 0)), back(full)]
        + [back(1), pl.BlockSpec((1, full), lambda i, *_: (0, 0))],
        [pltpu.VMEM((8, part), F32), pltpu.VMEM((TILE, part), F32)],
        flops=2 * row_count * full * part * 4,
    )


def front_terms(owners, left, right):
    row_count, depth = left.shape
    size = owners.shape[0]
    width = right.shape[1] // size

    def body(own_ref, l_ref, r_ref, *outs):
        for k in range(size):
            at = pl.ds(pl.multiple_of(own_ref[k] * width, width), width)
            term = jnp.dot(l_ref[...], r_ref[:, at], preferred_element_type=F32)
            outs[2 * k][...] = term[:, : width // 2].astype(BF)
            outs[2 * k + 1][...] = term[:, width // 2 :].astype(BF)

    return run(
        body,
        (row_count // BIG,),
        owners,
        [left, right],
        [tiles(depth, BIG), whole(right.shape)],
        [shape_of((row_count, width // 2), BF)] * (2 * size),
        [tiles(width // 2, BIG)] * (2 * size),
        flops=2 * row_count * depth * width * size,
    )


def add_low(left, right):
    return (left.astype(F32) + right.astype(F32)).astype(BF)


def scatter_plain(terms, axis):
    joined = jnp.concatenate([jnp.concatenate(pair, axis=1) for pair in terms], axis=axis).astype(F32)
    return lax.psum_scatter(joined, "narrow", scatter_dimension=axis, tiled=True)


def total_of(pairs):
    return jnp.concatenate(
        [functools.reduce(jnp.add, [pair[k].astype(F32) for pair in pairs]) for k in (0, 1)], axis=1
    )


def wide_all(block, axis):
    return lax.all_gather(block, "wide", axis=axis, tiled=True)


def wide_sums(terms, axis):
    return lax.psum_scatter(terms.astype(BF), "wide", scatter_dimension=axis, tiled=True)


def narrow_total(values):
    return lax.psum(values, "narrow")


def to_core_sum(values):
    return values + to_core(values)


def line_total(values, beside):
    others = [lax.ppermute(values, "wide", [(i, i ^ bit) for i in range(8)]) for bit in (2, 4, 6)]
    others, done = lax.optimization_barrier((others, beside()))
    return functools.reduce(jnp.add, others, values), done


def to_core(values):
    return lax.ppermute(values, "wide", [(i, i ^ 1) for i in range(lax.axis_size("wide"))])


def line_step(state, step):
    sums, right, left = state
    z = lax.axis_index("wide") // 2

    def with_own(come, chip):
        own = lax.dynamic_index_in_dim(sums, jnp.clip(chip, 0, 3), 0, keepdims=False)
        return own if come is None else add_low(own, come)

    return (
        sums,
        lax.ppermute(with_own(right, z + 4 - step), "wide", [(w, w + 2) for w in range(2 * step)]),
        lax.ppermute(with_own(left, z - 4 + step), "wide", [(w, w - 2) for w in range(8 - 2 * step, 8)]),
    )


def line_sums(terms, core):
    blocks = terms.reshape(4, 2, terms.shape[0] // 8, terms.shape[1])
    other = to_core(lax.dynamic_index_in_dim(blocks, 1 - core, 1, keepdims=False))
    return add_low(lax.dynamic_index_in_dim(blocks, core, 1, keepdims=False), other)


def line_end(state):
    sums, right, left = line_step(state, 3)
    own = lax.dynamic_index_in_dim(sums, lax.axis_index("wide") // 2, 0, keepdims=False)
    return own.astype(F32) + right.astype(F32) + left.astype(F32)


def after(value, *others):
    return lax.optimization_barrier((value, *others))[0]


def per_device(
    square,
    size,
    tokens,
    segment_ids,
    norm1_gain,
    in_weight,
    conv_weight,
    out_weight,
    norm2_gain,
    gate_weight,
    up_weight,
    down_weight,
    cotangent,
):
    full_width = norm1_gain.shape[0]
    part_width = tokens.shape[1]
    units = gate_weight.shape[1]
    row_count = tokens.shape[0]
    band = row_count // size
    me = lax.axis_index("narrow")
    core = lax.axis_index("wide") % 2
    me_s = me.reshape(1).astype(jnp.int32)
    core_s = core.reshape(1).astype(jnp.int32)
    offset = me * part_width
    kernel = lax.dynamic_slice_in_dim(conv_weight, offset, part_width, 1)
    gain_one, gain_two = norm1_gain[None, :], norm2_gain[None, :]

    order = [me ^ 3, me ^ 1, me ^ 2, me] if square else list(range(size))
    owners = jnp.stack([jnp.asarray(o, jnp.int32) for o in order])

    positions = lax.broadcasted_iota(jnp.int32, (row_count,), 0)
    masks = jnp.stack(
        [((positions >= k) & (segment_ids == lagged(segment_ids, k))).astype(F32) for k in (1, 2)], axis=1
    )
    barrier = lax.optimization_barrier
    in_cols = 3 * part_width
    pack = [in_weight[:, k] for k in range(3)]
    both = jnp.concatenate([gate_weight, up_weight], axis=1)

    def project_rows(x_pieces, in_all):
        return tuple(project(me_s, x_pieces, square, gain_one, in_all, kernel, masks))

    def unpacked(in_all):
        rows = in_all[:, in_cols:].reshape(-1, pack[0].shape[0], 2, part_width // 2)
        return rows.transpose(2, 1, 0, 3).reshape(part_width, full_width)

    if square:
        in_all = wide_all(packed_block(in_weight.transpose(1, 0, 2), out_weight), 0)
        x_pieces = gather_pieces(tokens, 1, True)[0]
        both_all = wide_all(after(both, *x_pieces), 0)

        half_cols = full_width // 2
        own_out = lax.dynamic_slice(in_all, (core * half_cols, jnp.int32(in_cols)), (half_cols, part_width))
        low_grad, high_grad = cotangent[:, : part_width // 4], cotangent[:, part_width // 4 :]
        x_out, y_out, low_far, projected = barrier(
            (to_x(own_out), to_y(own_out), to_far(after(low_grad, *x_pieces)), project_rows(x_pieces, in_all))
        )
        normed_one, x_full, mixed, filtered, mixer_low, scale_one = projected
        down_all = wide_all(after(down_weight, mixer_low), 1)
        x_mix, y_mix = barrier((to_x(mixer_low), to_y(mixer_low)))
        low_out, high_out = to_x(halves(y_out, 0)[0]), to_y(halves(x_out, 0)[1])
        low_mix, high_mix, low_out, high_out, *near = barrier(
            (
                to_x(halves(y_mix, 1)[0]),
                to_y(halves(x_mix, 1)[1]),
                low_out,
                high_out,
                to_core(own_out),
                to_core(x_out),
                to_core(y_out),
            )
        )
        far = [to_core(low_out), to_core(high_out)]
        y_pieces = [mixer_low, x_mix, y_mix, low_mix, high_mix]
        mine, other = [own_out, x_out, y_out, low_out, high_out], [*near, *far]
        grad_now, high_now, _ = barrier((cotangent, high_grad, low_mix))
        hidden, normed_two, scale_two = mix(core_s, y_pieces, mine, other, x_full, gain_two)
        x_grad, y_grad, high_far, (hidden_low, slope_up, slope_gate) = barrier(
            (to_x(grad_now), to_y(grad_now), to_far(high_now), expand(me_s, normed_two, both_all))
        )
        g_pieces = [cotangent, x_grad, y_grad, low_far, high_far]
    else:
        in_all = wide_all(jnp.concatenate(pack, axis=1), 0)
        out_rows = wide_all(out_weight, 1)
        x_pieces = gather_pieces(tokens, 1, False)[0]
        both_all = wide_all(both, 0)
        down_all = wide_all(down_weight, 1)
        normed_one, x_full, mixed, filtered, mixer_low, scale_one = project_rows(x_pieces, in_all)
        y_pieces = gather_pieces(mixer_low, 1, False)[0]
        mine, other = [lax.all_gather(out_rows, "narrow", axis=0, tiled=True)], []
        hidden, normed_two, scale_two = mix(core_s, y_pieces, mine, other, x_full, gain_two)
        hidden_low, slope_up, slope_gate = expand(me_s, normed_two, both_all)
        g_pieces = gather_pieces(cotangent, 1, False)[0]
    grad_full = lay(me_s, g_pieces, square)
    down_terms = contract_rows(hidden_low, grad_full).astype(BF)
    down_grad = wide_sums(down_terms, 1)
    slope_up = after(slope_up, down_terms)

    def ffn(which, d_both):
        *parts, d_gate, d_up = ffn_back(which, band, grad_full, slope_up, slope_gate, down_all, both_all, d_both)
        return list(zip(parts[0::2], parts[1::2])), (d_gate, d_up)

    def mixer(dh_pieces, out_rows):
        *parts, d_flat, kernel_grad, d_hidden_low, inner_one, gain_one_terms = mixer_back(
            owners, dh_pieces, out_rows, mixed, filtered, kernel, masks, in_all, x_full, scale_one, gain_one
        )
        inner_one = inner_one.reshape(-1, 128)
        return list(zip(parts[0::2], parts[1::2])), d_flat, kernel_grad, d_hidden_low, inner_one, gain_one_terms

    def dh_of(sums):
        return hidden_back(me_s, sums, hidden, scale_two, grad_full, gain_two)

    def tokens_grad_of(d_normed_one, inner_one, d_hidden_low):
        my_gain = lax.dynamic_slice_in_dim(norm1_gain, offset, part_width)
        inner_one = inner_one.reshape(row_count, 1) / full_width
        return (
            lax.dynamic_slice_in_dim(d_hidden_low, offset, part_width, 1).astype(F32)
            + scale_one * (d_normed_one * my_gain - tokens.astype(F32) * scale_one * scale_one * inner_one)
        ).astype(BF)

    def small_of(gain_terms, kernel_grad):
        return jnp.concatenate([lax.dynamic_index_in_dim(gain_terms, me, 1, keepdims=False), kernel_grad], axis=0)

    def out_terms_of(hidden_low):
        parts = front_terms(owners, hidden_low, down_all)
        return list(zip(parts[0::2], parts[1::2]))

    if square:
        (across, for_x), d_both = ffn(owners[:2], None)
        via_x, via_y, ((for_y,), d_both) = barrier((to_x(across[0]), to_y(across[1]), ffn(owners[2:3], d_both)))
        x_low, y_high, x_high, y_low, ((own,), d_both) = barrier(
            (
                to_x(after(for_x[0], via_x)),
                to_y(for_y[1]),
                add_low(for_x[1], via_y),
                add_low(for_y[0], via_x),
                ffn(owners[3:], d_both),
            )
        )
        x_high, y_low, gate_terms = barrier(
            (to_x(x_high), to_y(y_low), contract_rows(normed_two, d_both[0]).astype(BF))
        )
        gate_grad = wide_sums(gate_terms, 0)
        y_high = after(y_high, down_grad)
        d_hidden_rows, gain_two_terms = dh_of([own, (x_low, x_high), (y_low, y_high)])

        def beside_dh():
            up_terms = contract_rows(after(normed_two, d_hidden_rows), d_both[1]).astype(BF)
            return up_terms, unpacked(after(in_all, d_hidden_rows))

        dh_pieces, (up_terms, out_rows), out_parts = gather_pieces(
            d_hidden_rows, 0, True, (beside_dh, lambda first: out_terms_of(after(hidden_low, first[0])))
        )
        up_grad = wide_sums(up_terms, 0)
        out_parts, gate_grad = barrier((out_parts, gate_grad))
        out_first = [tuple(after(half, *dh_pieces[3:]) for half in part) for part in out_parts]
        out_via_x, out_via_y, out_x_low, out_y_high, mixer_outs = barrier(
            (
                to_x(out_first[0][0]),
                to_y(out_first[0][1]),
                to_x(out_first[1][0]),
                to_y(out_first[2][1]),
                mixer(dh_pieces, out_rows),
            )
        )
        one_parts, d_flat, kernel_grad, d_hidden_low, inner_one, gain_one_terms = mixer_outs
        gain_terms = jnp.concatenate([gain_one_terms, gain_two_terms], axis=0).reshape(2, size, part_width)
        via_x, via_y, x_inner, x_gain, in_terms = barrier(
            (
                to_x(one_parts[0][0]),
                to_y(one_parts[0][1]),
                to_x(inner_one),
                to_x(gain_terms),
                contract_rows(normed_one, d_flat).astype(BF),
            )
        )
        inner_one, gain_terms = inner_one + x_inner, gain_terms + x_gain
        x_low, y_high, y_inner, y_gain, x_high, y_low, out_x_high, out_y_low, out_terms, in_terms, up_grad = barrier(
            (
                to_x(after(one_parts[1][0], via_x)),
                to_y(after(one_parts[2][1], via_y)),
                to_y(inner_one),
                to_y(gain_terms),
                add_low(one_parts[1][1], via_y),
                add_low(one_parts[2][0], via_x),
                add_low(out_parts[1][1], out_via_y),
                add_low(out_parts[2][0], out_via_x),
                contract_rows(after(d_hidden_low, in_terms), mixer_low).astype(BF),
                in_terms,
                up_grad,
            )
        )
        in_grad = wide_sums(in_terms, 0)
        inner_one, gain_terms = inner_one + y_inner, gain_terms + y_gain
        x_high, y_low, line, small = barrier(
            (
                to_x(x_high),
                to_y(y_low),
                line_step((line_sums(out_terms, core), None, None), 1),
                to_core_sum(small_of(gain_terms, kernel_grad)),
            )
        )
        d_normed_one = total_of([one_parts[3], (x_low, x_high), (y_low, y_high)])
        tokens_grad = tokens_grad_of(d_normed_one, inner_one, d_hidden_low)
        small, (out_x_high, out_y_low, line) = line_total(
            small,
            lambda: (
                to_x(after(out_x_high, x_low, x_high)),
                to_y(after(out_y_low, y_low, y_high)),
                line_step(line, 2),
            ),
        )
        out_grad = line_end(line).T
        ffn_out = total_of([out_parts[3], (out_x_low, out_x_high), (out_y_low, out_y_high)])
    else:
        ffn_terms, d_both = ffn(owners, None)
        gate_grad, up_grad = [wide_sums(contract_rows(normed_two, d), 0) for d in d_both]
        d_hidden_rows, gain_two_terms = dh_of([tuple(halves(scatter_plain(ffn_terms, 0), 1))])
        one_parts, d_flat, kernel_grad, d_hidden_low, inner_one, gain_one_terms = mixer(
            gather_pieces(d_hidden_rows, 0, False)[0], out_rows
        )
        tokens_grad = tokens_grad_of(scatter_plain(one_parts, 1), narrow_total(inner_one), d_hidden_low)
        gain_terms = jnp.concatenate([gain_one_terms, gain_two_terms], axis=0).reshape(2, size, part_width)
        small = lax.psum(small_of(narrow_total(gain_terms), kernel_grad), "wide")
        ffn_out = scatter_plain(out_terms_of(hidden_low), 1)
        in_grad = wide_sums(contract_rows(normed_one, d_flat), 0)
        out_grad = wide_sums(contract_rows(mixer_low, d_hidden_low), 1)
    in_grad = jnp.stack([in_grad[:, k * part_width : (k + 1) * part_width] for k in range(3)], axis=1)
    block_out = (lax.dynamic_slice_in_dim(hidden, offset, part_width, 1) + ffn_out).astype(BF)
    gain_one_grad, gain_two_grad, kernel_grad = small[0], small[1], small[2:]
    return (
        block_out,
        tokens_grad,
        gain_one_grad,
        in_grad.astype(F32),
        kernel_grad,
        out_grad.astype(F32),
        gain_two_grad,
        gate_grad.astype(F32),
        up_grad.astype(F32),
        down_grad.astype(F32),
    )


def solution(mesh):
    size = mesh.shape["narrow"]
    square = size == 4 and mesh.shape["wide"] == 8

    def step(*args):
        return per_device(square, size, *args)

    in_specs = (
        P("wide", "narrow"),
        P("wide"),
        P(),
        P("wide", None, "narrow"),
        P(),
        P("narrow", "wide"),
        P(),
        P("wide", "narrow"),
        P("wide", "narrow"),
        P("narrow", "wide"),
        P("wide", "narrow"),
    )
    out_specs = (
        P("wide", "narrow"),
        P("wide", "narrow"),
        P("narrow"),
        P("wide", None, "narrow"),
        P(None, "narrow"),
        P("narrow", "wide"),
        P("narrow"),
        P("wide", "narrow"),
        P("wide", "narrow"),
        P("narrow", "wide"),
    )
    return jax.shard_map(step, mesh=mesh, in_specs=in_specs, out_specs=out_specs, check_vma=False)
```

```python
import functools

import jax
import jax.numpy as jnp
from jax import lax
from jax.experimental import pallas as pl
from jax.experimental.pallas import tpu as pltpu
from jax.sharding import PartitionSpec as P

CONV = 3
EPSILON = 1e-05
BF = jnp.bfloat16
F32 = jnp.float32
TILE = 512
BIG = 512


def contract_rows(left, right):
    return lax.dot_general(left, right, (((0,), (0,)), ((), ())), preferred_element_type=F32)


def contract_cols(left, right):
    return lax.dot_general(left, right, (((1,), (1,)), ((), ())), preferred_element_type=F32)


def lagged(values, shift_by):
    head = jnp.zeros((shift_by,) + values.shape[1:], values.dtype)
    return jnp.concatenate([head, values[: values.shape[0] - shift_by]], axis=0)


ALONG_X = [(0, 1), (1, 0), (2, 3), (3, 2)]
ALONG_Y = [(0, 2), (2, 0), (1, 3), (3, 1)]
ACROSS = [(0, 3), (3, 0), (1, 2), (2, 1)]


def to_x(values):
    return lax.ppermute(values, "narrow", ALONG_X)


def to_y(values):
    return lax.ppermute(values, "narrow", ALONG_Y)


def to_far(values):
    return lax.ppermute(values, "narrow", ACROSS)


def halves(values, axis):
    middle = values.shape[axis] // 2
    return lax.slice_in_dim(values, 0, middle, axis=axis), lax.slice_in_dim(values, middle, None, axis=axis)


def gather_pieces(block, axis, square, beside=(lambda: (), lambda _: ())):
    if not square:
        first = beside[0]()
        return [lax.all_gather(block, "narrow", axis=axis, tiled=True)], first, beside[1](first)
    from_x, from_y, first = lax.optimization_barrier((to_x(block), to_y(block), beside[0]()))
    low, high, second = lax.optimization_barrier(
        (to_x(halves(from_y, axis)[0]), to_y(halves(from_x, axis)[1]), beside[1](first))
    )
    return [block, from_x, from_y, low, high], first, second


def piece_starts(me, width, square):
    if not square:
        return [0]
    return [me * width, (me ^ 1) * width, (me ^ 2) * width, (me ^ 3) * width, (me ^ 3) * width + width // 2]


def whole(shape):
    return pl.BlockSpec(shape, lambda *_: (0,) * len(shape), pipeline_mode=pl.Buffered(1))


def tiles(width, tile=TILE):
    return pl.BlockSpec((tile, width), lambda i, *_: (i, 0))


def run(kernel, grid, scalars, operands, in_specs, outs, out_specs, scratch=(), flops=0, aliases=None, vmem=56):
    moved = sum(o.size * o.dtype.itemsize for o in operands) + sum(o.size * o.dtype.itemsize for o in outs)
    return pl.pallas_call(
        kernel,
        grid_spec=pltpu.PrefetchScalarGridSpec(
            num_scalar_prefetch=1, grid=grid, in_specs=in_specs, out_specs=out_specs, scratch_shapes=list(scratch)
        ),
        out_shape=outs,
        input_output_aliases=aliases or {},
        cost_estimate=pl.CostEstimate(flops=flops, bytes_accessed=moved, transcendentals=0),
        compiler_params=pltpu.CompilerParams(
            dimension_semantics=("arbitrary",) * len(grid), vmem_limit_bytes=vmem << 20
        ),
    )(scalars, *operands)


def shape_of(shape, dtype):
    return jax.ShapeDtypeStruct(shape, dtype)


def packed_block(in_parts, out_block):
    slim, part = in_parts.shape[1:]

    def body(_, in_ref, out_ref, o_ref):
        for k in range(3):
            o_ref[:, k * part : (k + 1) * part] = in_ref[k]
        for k in range(2):
            at = 3 * part + k * (part // 2)
            o_ref[:, at : at + part // 2] = out_ref[k * slim : (k + 1) * slim, :]

    return run(
        body,
        (1,),
        jnp.zeros((1,), jnp.int32),
        [in_parts, out_block],
        [whole(in_parts.shape), whole(out_block.shape)],
        [shape_of((slim, 4 * part), BF)],
        [whole((slim, 4 * part))],
        vmem=16,
    )[0]


def project(me, pieces, square, gain, weight, kernel, masks):
    count = len(pieces)
    row_count = pieces[0].shape[0]
    full, part = weight.shape[0], kernel.shape[1]
    share = full // (4 if square else 1)
    packed = pl.BlockSpec((full, 3 * part), lambda *_: (0, 0), pipeline_mode=pl.Buffered(1))

    def body(me_ref, *refs):
        xs, (gain_ref, w_ref, k_ref, m_ref), (n_ref, x_ref, p_ref, v_ref, y_ref, s_ref), (carry,) = (
            refs[:count],
            refs[count : count + 4],
            refs[count + 4 : count + 10],
            refs[count + 10 :],
        )

        @pl.when(pl.program_id(0) == 0)
        def _():
            carry[...] = jnp.zeros_like(carry)

        values = [ref[...].astype(F32) for ref in xs]
        total = functools.reduce(jnp.add, [jnp.sum(v * v, axis=1, keepdims=True) for v in values])
        scale = lax.rsqrt(total / full + EPSILON)
        s_ref[...] = scale
        for ref, v, start in zip(xs, values, piece_starts(me_ref[0], share, square)):
            at = pl.ds(pl.multiple_of(start, 128), v.shape[1])
            n_ref[:, at] = (v * scale * gain_ref[:, at]).astype(BF)
            x_ref[:, at] = ref[...]
        mixed = jnp.dot(n_ref[...], w_ref[...], preferred_element_type=F32)
        p_ref[...] = mixed
        gated = mixed[:, :part] * mixed[:, 2 * part :]
        row = lax.broadcasted_iota(jnp.int32, gated.shape, 0)
        before, last = carry[6:7, :], carry[7:8, :]
        back_one = jnp.where(row == 0, last, pltpu.roll(gated, 1, 0))
        back_two = jnp.where(row == 0, before, jnp.where(row == 1, last, pltpu.roll(gated, 2, 0)))
        carry[...] = gated[-8:, :]
        keep = m_ref[...]
        filtered = (
            k_ref[0:1, :] * gated + k_ref[1:2, :] * keep[:, 0:1] * back_one + k_ref[2:3, :] * keep[:, 1:2] * back_two
        )
        v_ref[...] = filtered
        y_ref[...] = (mixed[:, part : 2 * part] * filtered).astype(BF)

    return run(
        body,
        (row_count // TILE,),
        me,
        [*pieces, gain, weight, kernel, masks],
        [tiles(p.shape[1]) for p in pieces] + [whole(gain.shape), packed, whole(kernel.shape), tiles(2)],
        [
            shape_of((row_count, full), BF),
            shape_of((row_count, full), BF),
            shape_of((row_count, 3 * part), F32),
            shape_of((row_count, part), F32),
            shape_of((row_count, part), BF),
            shape_of((row_count, 1), F32),
        ],
        [tiles(full), tiles(full), tiles(3 * part), tiles(part), tiles(part), tiles(1)],
        [pltpu.VMEM((8, part), F32)],
        flops=2 * row_count * full * 3 * part,
    )


def mix(core, pieces, mine, other, x_full, gain):
    count = len(pieces)
    row_count, full = x_full.shape
    packed = bool(other)
    mats = [*mine, *other]
    parts = len(mats)
    slab = pieces[0].shape[1] // 2

    def body(core_ref, *refs):
        ys, ms, (x_ref, gain_ref), (h_ref, n_ref, s_ref), (all_ref, *weight) = (
            refs[:count],
            refs[count : count + parts],
            refs[count + parts : count + parts + 2],
            refs[count + parts + 2 : count + parts + 5],
            refs[count + parts + 5 :],
        )
        weight_ref = weight[0] if packed else ms[0]

        if packed:

            @pl.when(pl.program_id(0) == 0)
            def _():
                for side in range(2):
                    start = (core_ref[0] ^ side) * (full // 2)
                    for k in range(5):
                        ref = ms[5 * side + k]
                        for n in range(ref.shape[0] // slab):
                            column = start + (n + (k == 4) * (full // 4 // slab)) * slab
                            at = pl.ds(pl.multiple_of(column, 128), slab)
                            for half in range(2):
                                row = (2 * min(k, 3) + half) * slab
                                weight_ref[row : row + slab, at] = ref[
                                    n * slab : (n + 1) * slab, half * slab : (half + 1) * slab
                                ]

        at = 0
        for ref in ys:
            all_ref[:, at : at + ref.shape[1]] = ref[...]
            at += ref.shape[1]
        h = x_ref[...].astype(F32) + jnp.dot(all_ref[...], weight_ref[...], preferred_element_type=F32)
        h_ref[...] = h
        scale = lax.rsqrt(jnp.sum(h * h, axis=1, keepdims=True) / full + EPSILON)
        s_ref[...] = scale
        n_ref[...] = (h * scale * gain_ref[...]).astype(BF)

    return run(
        body,
        (row_count // BIG,),
        core,
        [*pieces, *mats, x_full, gain],
        [tiles(p.shape[1], BIG) for p in pieces] + [whole(m.shape) for m in mats] + [tiles(full, BIG), whole(gain.shape)],
        [shape_of((row_count, full), F32), shape_of((row_count, full), BF), shape_of((row_count, 1), F32)],
        [tiles(full, BIG), tiles(full, BIG), tiles(1, BIG)],
        [pltpu.VMEM((BIG, full), BF)] + ([pltpu.VMEM((full, full), BF)] if packed else []),
        flops=2 * row_count * full * full,
    )


def lay(me, pieces, square):
    if not square:
        return pieces[0]
    row_count, share = pieces[0].shape
    full = 4 * share

    def body(me_ref, *refs):
        starts = piece_starts(me_ref[0], share, True)
        starts[4] = starts[3] + pieces[3].shape[1]
        for ref, start in zip(refs[:-1], starts):
            refs[-1][:, pl.ds(pl.multiple_of(start, 128), ref.shape[1])] = ref[...]

    return run(
        body,
        (row_count // BIG,),
        me,
        pieces,
        [tiles(p.shape[1], BIG) for p in pieces],
        [shape_of((row_count, full), BF)],
        [tiles(full, BIG)],
    )[0]


def expand(me, normed, weight):
    row_count, full = normed.shape
    units = weight.shape[1] // 2

    def body(_, n_ref, w_ref, q_ref, a_ref, b_ref):
        step = min(512, units)
        for at in range(0, units, step):
            gate = jnp.dot(n_ref[...], w_ref[:, at : at + step], preferred_element_type=F32)
            up = jnp.dot(n_ref[...], w_ref[:, units + at : units + at + step], preferred_element_type=F32)
            sig = 1.0 / (1.0 + jnp.exp(-gate))
            active = gate * sig
            q_ref[:, at : at + step] = (active * up).astype(BF)
            a_ref[:, at : at + step] = active.astype(BF)
            b_ref[:, at : at + step] = (up * sig * (1.0 + gate * (1.0 - sig))).astype(BF)

    return run(
        body,
        (row_count // BIG,),
        me,
        [normed, weight],
        [tiles(full, BIG), whole(weight.shape)],
        [shape_of((row_count, units), BF)] * 3,
        [tiles(units, BIG)] * 3,
        flops=2 * row_count * full * 2 * units,
    )


def ffn_back(owners, band, grad, slope_up, slope_gate, down, weight, d_both=None):
    bands = owners.shape[0]
    row_count, full = grad.shape
    units = down.shape[0]
    step = min(512, units)
    count = units // step

    def body(_, g_ref, a_ref, b_ref, d_ref, wg_ref, wu_ref, *refs):
        *halves_of, dg_ref, du_ref, total = refs[-2 * bands - 3 :]
        j = pl.program_id(1)
        dq = contract_cols(g_ref[...], d_ref[...])
        d_gate = (dq * b_ref[...].astype(F32)).astype(BF)
        d_up = (dq * a_ref[...].astype(F32)).astype(BF)
        dg_ref[...] = d_gate
        du_ref[...] = d_up
        term = contract_cols(d_gate, wg_ref[...]) + contract_cols(d_up, wu_ref[...])

        @pl.when(j == 0)
        def _():
            total[...] = term

        @pl.when(j > 0)
        def _():
            total[...] += term

        for k in range(bands):

            @pl.when((pl.program_id(0) == k) & (j == count - 1))
            def _(k=k):
                halves_of[2 * k][...] = total[:, : full // 2].astype(BF)
                halves_of[2 * k + 1][...] = total[:, full // 2 :].astype(BF)

    return run(
        body,
        (bands, count),
        owners,
        [grad, slope_up, slope_gate, down, weight, weight] + list(d_both or []),
        [
            pl.BlockSpec((band, full), lambda i, j, o: (o[i], 0)),
            pl.BlockSpec((band, step), lambda i, j, o: (o[i], j)),
            pl.BlockSpec((band, step), lambda i, j, o: (o[i], j)),
            pl.BlockSpec((step, full), lambda i, j, o: (j, 0)),
            pl.BlockSpec((full, step), lambda i, j, o: (0, j)),
            pl.BlockSpec((full, step), lambda i, j, o: (0, count + j)),
        ]
        + [pl.BlockSpec(memory_space=pl.ANY)] * len(d_both or []),
        [shape_of((band, full // 2), BF)] * (2 * bands) + [shape_of((row_count, units), BF)] * 2,
        [pl.BlockSpec((band, full // 2), lambda i, j, o: (0, 0))] * (2 * bands)
        + [pl.BlockSpec((band, step), lambda i, j, o: (o[i], j))] * 2,
        [pltpu.VMEM((band, full), F32)],
        flops=6 * bands * band * full * units,
        aliases={7: 2 * bands, 8: 2 * bands + 1} if d_both else None,
    )


def hidden_back(me, terms, hidden, scale_two, grad, gain):
    band = terms[0][0].shape[0]
    full = gain.shape[1]
    tile = min(128, band)
    count = 2 * len(terms)

    def body(_, *refs):
        h_ref, s_ref, g_ref, gain_ref, o_ref, n_ref = refs[count:]

        @pl.when(pl.program_id(0) == 0)
        def _():
            n_ref[...] = jnp.zeros_like(n_ref)

        sums = [functools.reduce(jnp.add, [r[...].astype(F32) for r in refs[k:count:2]]) for k in (0, 1)]
        d_normed = jnp.concatenate(sums, axis=1)
        h, scale = h_ref[...], s_ref[...]
        scaled = d_normed * gain_ref[...]
        inner = jnp.sum(scaled * h, axis=1, keepdims=True) / full
        o_ref[...] = (g_ref[...].astype(F32) + scale * (scaled - h * scale * scale * inner)).astype(BF)
        n_ref[...] += jnp.sum(d_normed * h * scale, axis=0, keepdims=True)

    def mine(width):
        return pl.BlockSpec((tile, width), lambda i, o: (o[0] * (band // tile) + i, 0))

    flat = [half for pair in terms for half in pair]
    return run(
        body,
        (band // tile,),
        me,
        [*flat, hidden, scale_two, grad, gain],
        [tiles(f.shape[1], tile) for f in flat] + [mine(full), mine(1), mine(full), whole(gain.shape)],
        [shape_of((band, full), BF), shape_of((1, full), F32)],
        [tiles(full, tile), pl.BlockSpec((1, full), lambda i, *_: (0, 0))],
    )


def mixer_back(owners, pieces, out_rows, mixed, filtered, kernel, masks, weight, x_full, scale_one, gain):
    part, full = out_rows.shape
    row_count = mixed.shape[0]
    count = row_count // TILE
    size = owners.shape[0]
    given = len(pieces)
    assert given == 1 or row_count == size * TILE
    packed = pl.BlockSpec((full, 3 * part), lambda *_: (0, 0), pipeline_mode=pl.Buffered(1))

    def body(own_ref, *refs):
        w_ref, p_ref, v_ref, k_ref, m_ref, r_ref, x_ref, s_ref, gain_ref = refs[given : given + 9]
        outs = refs[given + 9 : given + 9 + 2 * size]
        o_ref, kg_ref, d_ref, row_ref, g_ref, carry, dy_ref = refs[given + 9 + 2 * size :]
        i = pl.program_id(0)

        @pl.when(i == 0)
        def _():
            carry[...] = jnp.zeros_like(carry)
            kg_ref[...] = jnp.zeros_like(kg_ref)
            g_ref[...] = jnp.zeros_like(g_ref)

        first = (count - 1 - i) * TILE
        if given == 1:
            d_ref[...] = refs[0][pl.ds(pl.multiple_of(first, TILE), TILE), :]
        else:
            apart = (count - 1 - i) ^ own_ref[size - 1]
            for k in range(3):

                @pl.when(apart == k)
                def _(k=k):
                    d_ref[...] = refs[k][...]

            @pl.when(apart == 3)
            def _():
                d_ref[: TILE // 2, :] = refs[3][...]
                d_ref[TILE // 2 :, :] = refs[4][...]

        dy_ref[...] = contract_cols(d_ref[...], w_ref[...])
        dy = dy_ref[...]
        b, c, x = p_ref[:, :part], p_ref[:, part : 2 * part], p_ref[:, 2 * part :]
        dv = dy * c
        keep = m_ref[...]
        one, two = dv * keep[:, 0:1], dv * keep[:, 1:2]
        row = lax.broadcasted_iota(jnp.int32, dv.shape, 0)
        end = TILE - 1
        next_one = jnp.where(row == end, carry[0:1, :], pltpu.roll(one, TILE - 1, 0))
        next_two = jnp.where(
            row == end, carry[2:3, :], jnp.where(row == end - 1, carry[1:2, :], pltpu.roll(two, TILE - 2, 0))
        )
        carry[0:1, :] = one[0:1, :]
        carry[1:3, :] = two[0:2, :]
        u = b * x
        kg_ref[0:1, :] += jnp.sum(dv * u, axis=0, keepdims=True)
        kg_ref[1:2, :] += jnp.sum(next_one * u, axis=0, keepdims=True)
        kg_ref[2:3, :] += jnp.sum(next_two * u, axis=0, keepdims=True)
        du = k_ref[0:1, :] * dv + k_ref[1:2, :] * next_one + k_ref[2:3, :] * next_two
        o_ref[:, :part] = (du * x).astype(BF)
        o_ref[:, part : 2 * part] = (dy * v_ref[...]).astype(BF)
        o_ref[:, 2 * part :] = (du * b).astype(BF)
        total = 0.0
        for k in range(size):
            rows = pl.ds(pl.multiple_of(own_ref[k] * part, part), part)
            term = contract_cols(o_ref[...], r_ref[rows, :])
            by_x = term * x_ref[:, rows].astype(F32)
            total = total + jnp.sum(by_x * gain_ref[:, rows], axis=1, keepdims=True)
            g_ref[:, rows] += jnp.sum(by_x * s_ref[...], axis=0, keepdims=True)
            outs[2 * k][...] = term[:, : part // 2].astype(BF)
            outs[2 * k + 1][...] = term[:, part // 2 :].astype(BF)
        row_ref[...] = total

    def back(width):
        return pl.BlockSpec((TILE, width), lambda i, *_: (count - 1 - i, 0))

    return run(
        body,
        (count,),
        owners,
        [*pieces, out_rows, mixed, filtered, kernel, masks, weight, x_full, scale_one, gain],
        [whole(p.shape) for p in pieces]
        + [whole(out_rows.shape), back(3 * part), back(part), whole(kernel.shape), back(2), packed]
        + [back(full), back(1), whole(gain.shape)],
        [shape_of((row_count, part // 2), BF)] * (2 * size)
        + [shape_of((row_count, 3 * part), BF), shape_of((CONV, part), F32), shape_of((row_count, full), BF)]
        + [shape_of((row_count, 1), F32), shape_of((1, full), F32)],
        [back(part // 2)] * (2 * size)
        + [back(3 * part), pl.BlockSpec((CONV, part), lambda i, *_: (0, 0)), back(full)]
        + [back(1), pl.BlockSpec((1, full), lambda i, *_: (0, 0))],
        [pltpu.VMEM((8, part), F32), pltpu.VMEM((TILE, part), F32)],
        flops=2 * row_count * full * part * 4,
    )


def front_terms(owners, left, right):
    row_count, depth = left.shape
    size = owners.shape[0]
    width = right.shape[1] // size

    def body(own_ref, l_ref, r_ref, *outs):
        for k in range(size):
            at = pl.ds(pl.multiple_of(own_ref[k] * width, width), width)
            term = jnp.dot(l_ref[...], r_ref[:, at], preferred_element_type=F32)
            outs[2 * k][...] = term[:, : width // 2].astype(BF)
            outs[2 * k + 1][...] = term[:, width // 2 :].astype(BF)

    return run(
        body,
        (row_count // BIG,),
        owners,
        [left, right],
        [tiles(depth, BIG), whole(right.shape)],
        [shape_of((row_count, width // 2), BF)] * (2 * size),
        [tiles(width // 2, BIG)] * (2 * size),
        flops=2 * row_count * depth * width * size,
    )


def add_low(left, right):
    return (left.astype(F32) + right.astype(F32)).astype(BF)


def scatter_plain(terms, axis):
    joined = jnp.concatenate([jnp.concatenate(pair, axis=1) for pair in terms], axis=axis).astype(F32)
    return lax.psum_scatter(joined, "narrow", scatter_dimension=axis, tiled=True)


def total_of(pairs):
    return jnp.concatenate(
        [functools.reduce(jnp.add, [pair[k].astype(F32) for pair in pairs]) for k in (0, 1)], axis=1
    )


def wide_all(block, axis):
    return lax.all_gather(block, "wide", axis=axis, tiled=True)


def wide_sums(terms, axis):
    return lax.psum_scatter(terms.astype(BF), "wide", scatter_dimension=axis, tiled=True)


def narrow_total(values):
    return lax.psum(values, "narrow")


def to_core_sum(values):
    return values + to_core(values)


def line_total(values, beside):
    others = [lax.ppermute(values, "wide", [(i, i ^ bit) for i in range(8)]) for bit in (2, 4, 6)]
    others, done = lax.optimization_barrier((others, beside()))
    return functools.reduce(jnp.add, others, values), done


def to_core(values):
    return lax.ppermute(values, "wide", [(i, i ^ 1) for i in range(lax.axis_size("wide"))])


def line_step(state, step):
    sums, right, left = state
    z = lax.axis_index("wide") // 2

    def with_own(come, chip):
        own = lax.dynamic_index_in_dim(sums, jnp.clip(chip, 0, 3), 0, keepdims=False)
        return own if come is None else add_low(own, come)

    return (
        sums,
        lax.ppermute(with_own(right, z + 4 - step), "wide", [(w, w + 2) for w in range(2 * step)]),
        lax.ppermute(with_own(left, z - 4 + step), "wide", [(w, w - 2) for w in range(8 - 2 * step, 8)]),
    )


def line_sums(terms, core):
    blocks = terms.reshape(4, 2, terms.shape[0] // 8, terms.shape[1])
    other = to_core(lax.dynamic_index_in_dim(blocks, 1 - core, 1, keepdims=False))
    return add_low(lax.dynamic_index_in_dim(blocks, core, 1, keepdims=False), other)


def line_end(state):
    sums, right, left = line_step(state, 3)
    own = lax.dynamic_index_in_dim(sums, lax.axis_index("wide") // 2, 0, keepdims=False)
    return own.astype(F32) + right.astype(F32) + left.astype(F32)


def after(value, *others):
    return lax.optimization_barrier((value, *others))[0]


def per_device(
    square,
    size,
    tokens,
    segment_ids,
    norm1_gain,
    in_weight,
    conv_weight,
    out_weight,
    norm2_gain,
    gate_weight,
    up_weight,
    down_weight,
    cotangent,
):
    full_width = norm1_gain.shape[0]
    part_width = tokens.shape[1]
    units = gate_weight.shape[1]
    row_count = tokens.shape[0]
    band = row_count // size
    me = lax.axis_index("narrow")
    core = lax.axis_index("wide") % 2
    me_s = me.reshape(1).astype(jnp.int32)
    core_s = core.reshape(1).astype(jnp.int32)
    offset = me * part_width
    kernel = lax.dynamic_slice_in_dim(conv_weight, offset, part_width, 1)
    gain_one, gain_two = norm1_gain[None, :], norm2_gain[None, :]

    order = [me ^ 3, me ^ 1, me ^ 2, me] if square else list(range(size))
    owners = jnp.stack([jnp.asarray(o, jnp.int32) for o in order])

    positions = lax.broadcasted_iota(jnp.int32, (row_count,), 0)
    masks = jnp.stack(
        [((positions >= k) & (segment_ids == lagged(segment_ids, k))).astype(F32) for k in (1, 2)], axis=1
    )
    barrier = lax.optimization_barrier
    in_cols = 3 * part_width
    pack = [in_weight[:, k] for k in range(3)]
    both = jnp.concatenate([gate_weight, up_weight], axis=1)

    def project_rows(x_pieces, in_all):
        return tuple(project(me_s, x_pieces, square, gain_one, in_all, kernel, masks))

    def unpacked(in_all):
        rows = in_all[:, in_cols:].reshape(-1, pack[0].shape[0], 2, part_width // 2)
        return rows.transpose(2, 1, 0, 3).reshape(part_width, full_width)

    if square:
        in_all = wide_all(packed_block(in_weight.transpose(1, 0, 2), out_weight), 0)
        x_pieces = gather_pieces(tokens, 1, True)[0]
        both_all = wide_all(after(both, *x_pieces), 0)

        half_cols = full_width // 2
        own_out = lax.dynamic_slice(in_all, (core * half_cols, jnp.int32(in_cols)), (half_cols, part_width))
        low_grad, high_grad = cotangent[:, : part_width // 4], cotangent[:, part_width // 4 :]
        x_out, y_out, low_far, projected = barrier(
            (to_x(own_out), to_y(own_out), to_far(after(low_grad, *x_pieces)), project_rows(x_pieces, in_all))
        )
        normed_one, x_full, mixed, filtered, mixer_low, scale_one = projected
        down_all = wide_all(after(down_weight, mixer_low), 1)
        x_mix, y_mix = barrier((to_x(mixer_low), to_y(mixer_low)))
        low_out, high_out = to_x(halves(y_out, 0)[0]), to_y(halves(x_out, 0)[1])
        low_mix, high_mix, low_out, high_out, *near = barrier(
            (
                to_x(halves(y_mix, 1)[0]),
                to_y(halves(x_mix, 1)[1]),
                low_out,
                high_out,
                *[to_core(after(block, x_mix, y_mix)) for block in (own_out, x_out, y_out)],
            )
        )
        far = [to_core(low_out), to_core(high_out)]
        y_pieces = [mixer_low, x_mix, y_mix, low_mix, high_mix]
        mine, other = [own_out, x_out, y_out, low_out, high_out], [*near, *far]
        grad_now, high_now, _ = barrier((cotangent, high_grad, low_mix))
        hidden, normed_two, scale_two = mix(core_s, y_pieces, mine, other, x_full, gain_two)
        x_grad, y_grad, high_far, (hidden_low, slope_up, slope_gate) = barrier(
            (to_x(grad_now), to_y(grad_now), to_far(high_now), expand(me_s, normed_two, both_all))
        )
        g_pieces = [cotangent, x_grad, y_grad, low_far, high_far]
    else:
        in_all = wide_all(jnp.concatenate(pack, axis=1), 0)
        out_rows = wide_all(out_weight, 1)
        x_pieces = gather_pieces(tokens, 1, False)[0]
        both_all = wide_all(both, 0)
        down_all = wide_all(down_weight, 1)
        normed_one, x_full, mixed, filtered, mixer_low, scale_one = project_rows(x_pieces, in_all)
        y_pieces = gather_pieces(mixer_low, 1, False)[0]
        mine, other = [lax.all_gather(out_rows, "narrow", axis=0, tiled=True)], []
        hidden, normed_two, scale_two = mix(core_s, y_pieces, mine, other, x_full, gain_two)
        hidden_low, slope_up, slope_gate = expand(me_s, normed_two, both_all)
        g_pieces = gather_pieces(cotangent, 1, False)[0]
    grad_full = lay(me_s, g_pieces, square)
    down_terms = contract_rows(hidden_low, grad_full).astype(BF)
    down_grad = wide_sums(down_terms, 1)
    slope_up = after(slope_up, down_terms)

    def ffn(which, d_both):
        *parts, d_gate, d_up = ffn_back(which, band, grad_full, slope_up, slope_gate, down_all, both_all, d_both)
        return list(zip(parts[0::2], parts[1::2])), (d_gate, d_up)

    def mixer(dh_pieces, out_rows):
        *parts, d_flat, kernel_grad, d_hidden_low, inner_one, gain_one_terms = mixer_back(
            owners, dh_pieces, out_rows, mixed, filtered, kernel, masks, in_all, x_full, scale_one, gain_one
        )
        inner_one = inner_one.reshape(-1, 128)
        return list(zip(parts[0::2], parts[1::2])), d_flat, kernel_grad, d_hidden_low, inner_one, gain_one_terms

    def dh_of(sums):
        return hidden_back(me_s, sums, hidden, scale_two, grad_full, gain_two)

    def tokens_grad_of(d_normed_one, inner_one, d_hidden_low):
        my_gain = lax.dynamic_slice_in_dim(norm1_gain, offset, part_width)
        inner_one = inner_one.reshape(row_count, 1) / full_width
        return (
            lax.dynamic_slice_in_dim(d_hidden_low, offset, part_width, 1).astype(F32)
            + scale_one * (d_normed_one * my_gain - tokens.astype(F32) * scale_one * scale_one * inner_one)
        ).astype(BF)

    def small_of(gain_terms, kernel_grad):
        return jnp.concatenate([lax.dynamic_index_in_dim(gain_terms, me, 1, keepdims=False), kernel_grad], axis=0)

    def out_terms_of(hidden_low):
        parts = front_terms(owners, hidden_low, down_all)
        return list(zip(parts[0::2], parts[1::2]))

    if square:
        (across, for_x), d_both = ffn(owners[:2], None)
        via_x, via_y, ((for_y,), d_both) = barrier((to_x(across[0]), to_y(across[1]), ffn(owners[2:3], d_both)))
        x_low, y_high, x_high, y_low, ((own,), d_both) = barrier(
            (
                to_x(after(for_x[0], via_x)),
                to_y(for_y[1]),
                add_low(for_x[1], via_y),
                add_low(for_y[0], via_x),
                ffn(owners[3:], d_both),
            )
        )
        x_high, y_low, gate_terms = barrier(
            (to_x(x_high), to_y(y_low), contract_rows(normed_two, d_both[0]).astype(BF))
        )
        gate_grad = wide_sums(gate_terms, 0)
        y_high = after(y_high, down_grad)
        d_hidden_rows, gain_two_terms = dh_of([own, (x_low, x_high), (y_low, y_high)])

        def beside_dh():
            up_terms = contract_rows(after(normed_two, d_hidden_rows), d_both[1]).astype(BF)
            return up_terms, unpacked(after(in_all, d_hidden_rows))

        dh_pieces, (up_terms, out_rows), out_parts = gather_pieces(
            d_hidden_rows, 0, True, (beside_dh, lambda first: out_terms_of(after(hidden_low, first[0])))
        )
        up_grad = wide_sums(up_terms, 0)
        out_parts, gate_grad = barrier((out_parts, gate_grad))
        out_first = [tuple(after(half, *dh_pieces[3:]) for half in part) for part in out_parts]
        out_via_x, out_via_y, out_x_low, out_y_high, mixer_outs = barrier(
            (
                to_x(out_first[0][0]),
                to_y(out_first[0][1]),
                to_x(out_first[1][0]),
                to_y(out_first[2][1]),
                mixer(dh_pieces, out_rows),
            )
        )
        one_parts, d_flat, kernel_grad, d_hidden_low, inner_one, gain_one_terms = mixer_outs
        gain_terms = jnp.concatenate([gain_one_terms, gain_two_terms], axis=0).reshape(2, size, part_width)
        via_x, via_y, x_inner, x_gain, in_terms = barrier(
            (
                to_x(one_parts[0][0]),
                to_y(one_parts[0][1]),
                to_x(inner_one),
                to_x(gain_terms),
                contract_rows(normed_one, d_flat).astype(BF),
            )
        )
        inner_one, gain_terms = inner_one + x_inner, gain_terms + x_gain
        x_low, y_high, y_inner, y_gain, x_high, y_low, out_x_high, out_y_low, out_terms, in_terms, up_grad = barrier(
            (
                to_x(after(one_parts[1][0], via_x)),
                to_y(after(one_parts[2][1], via_y)),
                to_y(inner_one),
                to_y(gain_terms),
                add_low(one_parts[1][1], via_y),
                add_low(one_parts[2][0], via_x),
                add_low(out_parts[1][1], out_via_y),
                add_low(out_parts[2][0], out_via_x),
                contract_rows(after(d_hidden_low, in_terms), mixer_low).astype(BF),
                in_terms,
                up_grad,
            )
        )
        in_grad = wide_sums(in_terms, 0)
        inner_one, gain_terms = inner_one + y_inner, gain_terms + y_gain
        x_high, y_low, line, small = barrier(
            (
                to_x(x_high),
                to_y(y_low),
                line_step((line_sums(out_terms, core), None, None), 1),
                to_core_sum(small_of(gain_terms, kernel_grad)),
            )
        )
        d_normed_one = total_of([one_parts[3], (x_low, x_high), (y_low, y_high)])
        tokens_grad = tokens_grad_of(d_normed_one, inner_one, d_hidden_low)
        small, (out_x_high, out_y_low, line) = line_total(
            small,
            lambda: (
                to_x(after(out_x_high, x_low, x_high)),
                to_y(after(out_y_low, y_low, y_high)),
                line_step(line, 2),
            ),
        )
        out_grad = line_end(line).T
        ffn_out = total_of([out_parts[3], (out_x_low, out_x_high), (out_y_low, out_y_high)])
    else:
        ffn_terms, d_both = ffn(owners, None)
        gate_grad, up_grad = [wide_sums(contract_rows(normed_two, d), 0) for d in d_both]
        d_hidden_rows, gain_two_terms = dh_of([tuple(halves(scatter_plain(ffn_terms, 0), 1))])
        one_parts, d_flat, kernel_grad, d_hidden_low, inner_one, gain_one_terms = mixer(
            gather_pieces(d_hidden_rows, 0, False)[0], out_rows
        )
        tokens_grad = tokens_grad_of(scatter_plain(one_parts, 1), narrow_total(inner_one), d_hidden_low)
        gain_terms = jnp.concatenate([gain_one_terms, gain_two_terms], axis=0).reshape(2, size, part_width)
        small = lax.psum(small_of(narrow_total(gain_terms), kernel_grad), "wide")
        ffn_out = scatter_plain(out_terms_of(hidden_low), 1)
        in_grad = wide_sums(contract_rows(normed_one, d_flat), 0)
        out_grad = wide_sums(contract_rows(mixer_low, d_hidden_low), 1)
    in_grad = jnp.stack([in_grad[:, k * part_width : (k + 1) * part_width] for k in range(3)], axis=1)
    block_out = (lax.dynamic_slice_in_dim(hidden, offset, part_width, 1) + ffn_out).astype(BF)
    gain_one_grad, gain_two_grad, kernel_grad = small[0], small[1], small[2:]
    return (
        block_out,
        tokens_grad,
        gain_one_grad,
        in_grad.astype(F32),
        kernel_grad,
        out_grad.astype(F32),
        gain_two_grad,
        gate_grad.astype(F32),
        up_grad.astype(F32),
        down_grad.astype(F32),
    )


def solution(mesh):
    size = mesh.shape["narrow"]
    square = size == 4 and mesh.shape["wide"] == 8

    def step(*args):
        return per_device(square, size, *args)

    in_specs = (
        P("wide", "narrow"),
        P("wide"),
        P(),
        P("wide", None, "narrow"),
        P(),
        P("narrow", "wide"),
        P(),
        P("wide", "narrow"),
        P("wide", "narrow"),
        P("narrow", "wide"),
        P("wide", "narrow"),
    )
    out_specs = (
        P("wide", "narrow"),
        P("wide", "narrow"),
        P("narrow"),
        P("wide", None, "narrow"),
        P(None, "narrow"),
        P("narrow", "wide"),
        P("narrow"),
        P("wide", "narrow"),
        P("wide", "narrow"),
        P("narrow", "wide"),
    )
    return jax.shard_map(step, mesh=mesh, in_specs=in_specs, out_specs=out_specs, check_vma=False)
```
